256 devices in a mesh: band: 4 (over y_lo, core), tile: 64 (over y_hi, x, z).
Axes of the slice: x: 4, y: 4 (y_hi: 2, y_lo: 2; y = y_hi * 2 + y_lo), z: 8, core: 2. Of those that a mesh axis runs over, the one named last changes fastest.
Arguments:
- sketch: float32 [8, 4, 384, 128, 128], P(None, 'band', 'tile'), may hold values from -6 to 6
- diag_coef: float32 [4, 384, 128], P('band', 'tile'), may hold values from 1 to 2
- couple: float32 [4, 384, 128], P('band', 'tile'), may hold values from 0.3 to 0.8
- kernel: bfloat16 [8, 512, 4, 384, 128], P(None, None, 'band', 'tile'), may hold values from -0.0048828125 to 0.0048828125
- noise_prec: float32 [8, 512], replicated, may hold values from 0.5 to 4
Outputs:
- hessian_sketch: float32 [8, 4, 384, 128, 128], P(None, 'band', 'tile')
The draws below stay inside these ranges and needn't reach their ends.
All inputs are finite; a program needn't handle non-finite values.
Results may differ from the reference program's by a relative error of at most 0.0041.
Values may be sent and summed in bfloat16 or wider, within the bound.
A program may use at most 128 MiB of HBM per device.

```python
import math
import jax
import jax.numpy as jnp

NT = 8
S = 512
K = 128
COLS = 128
BANDS = 4
ROWS = 384
POINTS = 196608


def shard_levels(own_key, shape, cuts, low, top_value):
    def one(position, blocks):
        steps = jax.random.uniform(jax.random.fold_in(jax.random.fold_in(own_key, 6), position), (blocks,), jnp.float32, low / len(cuts), top_value / len(cuts))
        return jnp.repeat(jnp.exp(steps), shape[position] // blocks).reshape((-1,) + (1,) * (len(shape) - position - 1))

    loudness = one(*cuts[0])
    for cut in cuts[1:]:
        loudness = loudness * one(*cut)
    return loudness


def bell_draw(own_key, extent, scale, reach, pieces=(), held_as=jnp.bfloat16):
    entries = scale * jax.random.normal(own_key, extent, jnp.float32)
    if pieces:
        entries = entries * shard_levels(own_key, extent, pieces, -0.22, 0.18)
    return jnp.clip(entries, -reach, reach).astype(held_as)


def setup_inputs(seed: int = 0) -> dict:
    seeds = jax.random.split(jax.random.key(seed), 6)
    sketch = bell_draw(seeds[0], (NT, BANDS, ROWS, COLS, K), 1.0, 6.0, ((1, 4), (2, 64)), jnp.float32)
    diag_coef = jnp.clip(1.0 + 1.0 * jax.random.uniform(seeds[1], (BANDS, ROWS, COLS), jnp.float32) ** shard_levels(seeds[1], (BANDS, ROWS, COLS), ((0, 4), (1, 64)), -0.2, 0.2), 1.0, 2.0)
    couple = jnp.clip(0.3 + 0.5 * jax.random.uniform(seeds[2], (BANDS, ROWS, COLS), jnp.float32) ** shard_levels(seeds[2], (BANDS, ROWS, COLS), ((0, 4), (1, 64)), -0.2, 0.2), 0.3, 0.8)
    kernel = bell_draw(seeds[3], (NT, S, BANDS, ROWS, COLS), (NT * POINTS) ** -0.5, 0.0048828125, ((2, 4), (3, 64)))
    noise_prec = jnp.clip(jnp.exp(jax.random.uniform(seeds[4], (NT, S), jnp.float32, math.log(0.5), math.log(4.0))), 0.5, 4.0)
    return {"sketch": sketch, "diag_coef": diag_coef, "couple": couple, "kernel": kernel, "noise_prec": noise_prec}


def sweep(field, diag_coef, couple):
    dcf = diag_coef[None, :, :, :, None]
    cpl = couple[None, :, :, :, None]
    coupled = cpl * field
    padded = jnp.pad(coupled, ((0, 0), (0, 0), (1, 1), (1, 1), (0, 0)))
    beside = padded[:, :, 2:, 1:-1] + padded[:, :, :-2, 1:-1] + padded[:, :, 1:-1, 2:] + padded[:, :, 1:-1, :-2]
    return dcf * field - cpl * beside


def reference(sketch, diag_coef, couple, kernel, noise_prec):
    smoothed = sweep(sweep(sketch, diag_coef, couple), diag_coef, couple).astype(jnp.bfloat16)
    flat = smoothed.reshape(NT, POINTS, K)
    kflat = kernel.reshape(NT, S, POINTS)
    rows = []
    for step in range(NT):
        acc = jnp.zeros((S, K), jnp.float32)
        for lag in range(step + 1):
            acc = acc + jnp.dot(kflat[lag], flat[step - lag], preferred_element_type=jnp.float32)
        rows.append(acc)
    data = jnp.stack(rows)
    weighted = (data * noise_prec[:, :, None]).astype(jnp.bfloat16)
    grads = []
    for step in range(NT):
        acc = jnp.zeros((POINTS, K), jnp.float32)
        for lag in range(NT - step):
            acc = acc + jnp.dot(kflat[lag].T, weighted[step + lag], preferred_element_type=jnp.float32)
        grads.append(acc)
    adjoint = jnp.stack(grads).reshape(sketch.shape)
    return sweep(sweep(adjoint, diag_coef, couple), diag_coef, couple)
```

```python
import functools

import jax
import jax.numpy as jnp
from jax import lax
from jax.experimental import pallas as pl
from jax.experimental.pallas import tpu as pltpu
from jax.sharding import PartitionSpec as P

F32 = jnp.float32
BF16 = jnp.bfloat16
MESH = pl.DeviceIdType.MESH
COLS = 128
PAD = 8


def beside(ref, row):
    return ref[row, pl.ds(PAD - 1, COLS), :] + ref[row, pl.ds(PAD + 1, COLS), :]


def clear_pads(ref, rows):
    zero = jnp.zeros((PAD, ref.shape[2]), F32)
    for row in range(rows):
        ref[row, 0:PAD, :] = zero
        ref[row, PAD + COLS : 2 * PAD + COLS, :] = zero


def two_sweeps(rows, value, cpl, dia, coupled, again, swept, put):
    body = pl.ds(PAD, COLS)
    for j in range(rows + 4):
        coupled[j, body, :] = cpl[j] * value(j)
    for j in range(1, rows + 3):
        near = coupled[j - 1, body, :] + coupled[j + 1, body, :] + beside(coupled, j)
        once = dia[j - 1] * value(j) - cpl[j] * near
        swept[j - 1] = once
        again[j - 1, body, :] = cpl[j] * once
    for r in range(rows):
        q = r + 1
        near = again[q - 1, body, :] + again[q + 1, body, :] + beside(again, q)
        put(r, dia[q] * swept[q] - cpl[q + 1] * near)


class Place:
    def __init__(self, sizes):
        self.nyl, self.nyh, self.nx, self.nz = sizes
        self.tiles = self.nyh * self.nx * self.nz
        self.band = lax.axis_index("band")
        self.tile = lax.axis_index("tile")
        self.core = lax.rem(self.band, 2)
        self.z = lax.rem(self.tile, self.nz)
        self.plane = self.nyl * self.nyh * self.nx
        self.g = self.band // 2 * (self.nyh * self.nx) + self.tile // self.nz

    def twin(self):
        return (self.band + 1 - 2 * self.core, self.tile)

    def in_plane(self, d):
        g = lax.rem(self.g + d, self.plane)
        inner = self.nyh * self.nx
        return g, (g // inner * 2 + self.core, lax.rem(g, inner) * self.nz + self.z)

    def along_z(self, d):
        z = lax.rem(self.z + d, self.nz)
        return (self.band, self.tile - self.z + z)

    def row_neighbour(self, step):
        return (self.band, lax.rem(self.tile + step + self.tiles, self.tiles))


def remote(src, dst, send, recv, where):
    return pltpu.make_async_remote_copy(
        src_ref=src, dst_ref=dst, send_sem=send, recv_sem=recv, device_id=where, device_id_type=MESH
    )


def main_kernel(
    sizes,
    sketch_hbm, diag_ref, couple_ref, kern_hbm, prec_ref,
    adj_hbm, edge_hbm, coef_hbm,
    kv, kt, sk, stage, hin, smooth, total, pair_in, xsend, xin, zsend, zin, wsend, wgt, adj, edge_out,
    coef_in, cpl, dia, coupled, again, swept,
    load_sem, coef_send, coef_recv, halo_send, halo_recv, pair_send, pair_recv, x_send, x_recv,
    z_send, z_recv, g_send, g_recv, p_send, p_recv, edge_send, edge_recv, out_sem,
):
    here = Place(sizes)
    steps, rows, sensors, _ = kv.shape
    points = rows * COLS
    chunks = steps // 2
    half = sensors // 2
    piece = half // here.plane
    others = here.plane - 1
    zothers = here.nz - 1
    up, down = here.row_neighbour(-1), here.row_neighbour(1)
    has_up, has_down = here.tile > 0, here.tile < here.tiles - 1
    twin = here.twin()

    sketch_loads = [
        pltpu.make_async_copy(sketch_hbm.at[t, 0], sk.at[t], load_sem.at[t]) for t in range(steps)
    ]
    kern_loads = [
        pltpu.make_async_copy(kern_hbm.at[lag, 0], kv.at[lag], load_sem.at[steps + lag])
        for lag in range(steps)
    ]
    for load in sketch_loads:
        load.start()
    for load in kern_loads:
        load.start()

    barrier = pltpu.get_barrier_semaphore()
    greeted = [up, down, twin]
    greeted += [here.in_plane(d)[1] for d in range(1, here.plane)]
    greeted += [here.along_z(d) for d in range(1, here.nz)]
    for where in greeted:
        pl.semaphore_signal(barrier, inc=1, device_id=where, device_id_type=MESH)

    clear_pads(coupled, rows + 4)
    clear_pads(again, rows + 2)
    smooth[0] = jnp.zeros((points, COLS), BF16)
    wgt[steps] = jnp.zeros((sensors, COLS), BF16)
    adj[...] = jnp.zeros(adj.shape, F32)

    @pl.when(jnp.logical_not(has_up))
    def _():
        hin[:, 0] = jnp.zeros((steps, 2 * COLS, COLS), BF16)

    @pl.when(jnp.logical_not(has_down))
    def _():
        hin[:, 1] = jnp.zeros((steps, 2 * COLS, COLS), BF16)

    for t in range(2):
        sketch_loads[t].wait()
        stage[t, 0] = sk[t, 0:2].reshape(2 * COLS, COLS).astype(BF16)
        stage[t, 1] = sk[t, rows - 2 : rows].reshape(2 * COLS, COLS).astype(BF16)

    pl.semaphore_wait(barrier, len(greeted))

    def coef_copies(side, where):
        return [
            remote(ref, coef_in.at[side, i], coef_send.at[side, i], coef_recv.at[side, i], where)
            for i, ref in enumerate((couple_ref, diag_ref))
        ]

    def halo_copy(t, side, where):
        return remote(
            stage.at[t, 1 - side], hin.at[t, side], halo_send.at[t, side], halo_recv.at[t, side], where
        )

    def edge_copy(t, side, where):
        return remote(
            edge_out.at[t, 1 - side], edge_hbm.at[t, side], edge_send.at[t, side], edge_recv.at[t, side], where
        )

    def send_halos(t, copy):
        @pl.when(has_up)
        def _():
            copy(t, 1, up).start()

        @pl.when(has_down)
        def _():
            copy(t, 0, down).start()

    def wait_halos(t, copy):
        @pl.when(has_up)
        def _():
            copy(t, 0, up).wait_recv()
            copy(t, 1, up).wait_send()

        @pl.when(has_down)
        def _():
            copy(t, 1, down).wait_recv()
            copy(t, 0, down).wait_send()

    @pl.when(has_up)
    def _():
        for copy in coef_copies(1, up):
            copy.start()

    @pl.when(has_down)
    def _():
        for copy in coef_copies(0, down):
            copy.start()

    for t in range(steps):
        if t >= 2:
            sketch_loads[t].wait()
            stage[t, 0] = sk[t, 0:2].reshape(2 * COLS, COLS).astype(BF16)
            stage[t, 1] = sk[t, rows - 2 : rows].reshape(2 * COLS, COLS).astype(BF16)
        send_halos(t, halo_copy)

    def over_lanes(row):
        return jnp.broadcast_to(row, (COLS, COLS)).T

    for r in range(rows):
        cpl[r + 2] = over_lanes(couple_ref[r])
        dia[r + 1] = over_lanes(diag_ref[r])

    blank = jnp.zeros((COLS, COLS), F32)

    @pl.when(has_up)
    def _():
        for copy in coef_copies(0, up):
            copy.wait_recv()
        for copy in coef_copies(1, up):
            copy.wait_send()
        cpl[0] = over_lanes(coef_in[0, 0, rows - 2])
        cpl[1] = over_lanes(coef_in[0, 0, rows - 1])
        dia[0] = over_lanes(coef_in[0, 1, rows - 1])

    @pl.when(jnp.logical_not(has_up))
    def _():
        cpl[0] = blank
        cpl[1] = blank
        dia[0] = blank

    @pl.when(has_down)
    def _():
        for copy in coef_copies(1, down):
            copy.wait_recv()
        for copy in coef_copies(0, down):
            copy.wait_send()
        cpl[rows + 2] = over_lanes(coef_in[1, 0, 0])
        cpl[rows + 3] = over_lanes(coef_in[1, 0, 1])
        dia[rows + 1] = over_lanes(coef_in[1, 1, 0])

    @pl.when(jnp.logical_not(has_down))
    def _():
        cpl[rows + 2] = blank
        cpl[rows + 3] = blank
        dia[rows + 1] = blank

    coef_out = [
        pltpu.make_async_copy(cpl, coef_hbm.at[0 : rows + 4], out_sem.at[steps]),
        pltpu.make_async_copy(dia, coef_hbm.at[rows + 4 : 2 * rows + 6], out_sem.at[steps + 1]),
    ]
    for copy in coef_out:
        copy.start()

    my_half = pl.multiple_of(here.core * half, half)
    twin_half = pl.multiple_of(half - here.core * half, half)
    my_piece = pl.multiple_of(here.g * piece, piece)
    my_sensors = pl.multiple_of(here.core * half + here.g * piece, piece)

    def smooth_step(t):
        wait_halos(t, halo_copy)

        def value(j):
            if j < 2:
                return hin[t, 0, j * COLS : (j + 1) * COLS, :].astype(F32)
            if j < rows + 2:
                return sk[t, j - 2]
            j = j - rows - 2
            return hin[t, 1, j * COLS : (j + 1) * COLS, :].astype(F32)

        def put(r, field):
            smooth[t + 1, r * COLS : (r + 1) * COLS, :] = field.astype(BF16)

        two_sweeps(rows, value, cpl, dia, coupled, again, swept, put)

    def pair_copy(c):
        return remote(
            total.at[c, pl.ds(twin_half, half)], pair_in.at[c], pair_send.at[c], pair_recv.at[c], twin
        )

    def forward(c):
        for t in (2 * c, 2 * c + 1):
            kern_loads[t].wait()

        def per_step(t, carry):
            smooth_step(t)
            return carry

        lax.fori_loop(2 * c, 2 * c + 2, per_step, 0)
        total[c] = jnp.zeros((sensors, 2 * COLS), F32)

        def per_lag(lag, carry):
            lhs = jnp.concatenate([kv[lag, r] for r in range(rows)], axis=1)
            rhs = jnp.concatenate([smooth[2 * c - lag + 1], smooth[2 * c - lag + 2]], axis=1)
            total[c] += jnp.dot(lhs, rhs, preferred_element_type=F32)
            return carry

        lax.fori_loop(0, 2 * c + 2, per_lag, 0)
        pair_copy(c).start()

    def plane_copies(c):
        copies = []
        for d in range(1, here.plane):
            g, where = here.in_plane(d)
            copies.append(
                remote(
                    xsend.at[c, pl.ds(pl.multiple_of(g * piece, piece), piece)],
                    xin.at[c, pl.ds((d - 1) * piece, piece)],
                    x_send.at[c], x_recv.at[c], where,
                )
            )
        return copies

    def bulk(c, send, recv):
        block = xin.at[c]
        return remote(block, block, send, recv, twin)

    def to_plane(c):
        pair_copy(c).wait()
        xsend[c] = (total[c, pl.ds(my_half, half)] + pair_in[c]).astype(BF16)
        for copy in plane_copies(c):
            copy.start()

    def z_copies(c):
        return [
            remote(zsend.at[c], zin.at[c, d - 1], z_send.at[c, d], z_recv.at[c, d], here.along_z(d))
            for d in range(1, here.nz)
        ]

    def own_sum(c):
        rows_here = pl.ds(pl.multiple_of(my_half + my_piece, piece), piece)
        acc = total[c, rows_here] + pair_in[c, pl.ds(my_piece, piece)]
        for d in range(others):
            acc = acc + xin[c, d * piece : (d + 1) * piece].astype(F32)
        return acc

    def to_z(c):
        bulk(c, x_send.at[c], x_recv.at[c]).wait()
        mine = own_sum(c)
        zin[c, zothers] = mine.astype(BF16)
        zsend[c] = mine.astype(BF16)
        for copy in z_copies(c):
            copy.start()

    def gather_copies(c):
        return [
            remote(
                wsend.at[c],
                wgt.at[pl.ds(2 * c, 2), pl.ds(my_sensors, piece)],
                g_send.at[c], g_recv.at[c], here.in_plane(d)[1],
            )
            for d in range(1, here.plane)
        ]

    spot = lax.broadcasted_iota(jnp.int32, (piece, sensors), 1)
    wanted = lax.broadcasted_iota(jnp.int32, (piece, sensors), 0) + my_sensors

    def to_gather(c):
        for copy in z_copies(c):
            copy.wait()
        acc = own_sum(c)
        for d in range(zothers):
            acc = acc + zin[c, d].astype(F32)
        for i in range(2):
            t = 2 * c + i
            scale = jnp.sum(
                jnp.where(spot == wanted, prec_ref[t : t + 1, :], 0.0), axis=1, keepdims=True
            )
            block = (acc[:, i * COLS : (i + 1) * COLS] * scale).astype(BF16)
            wsend[c, i] = block
            wgt[t, pl.ds(my_sensors, piece), :] = block
        for copy in gather_copies(c):
            copy.start()

    def twin_copy(c):
        block = wgt.at[pl.ds(2 * c, 2), pl.ds(my_half, half)]
        return remote(block, block, p_send.at[c], p_recv.at[c], twin)

    def to_twin(c):
        bulk(c, g_send.at[c], g_recv.at[c]).wait()
        twin_copy(c).start()

    def flip(lag, carry):
        for r in range(rows):
            kt[lag, r * COLS : (r + 1) * COLS, :] = kv[lag, r].T
        return carry

    def back(c, low, high):
        def per_lag(lag, carry):
            rhs = jnp.concatenate([wgt[2 * c + lag], wgt[2 * c + lag + 1]], axis=1)
            out = jnp.dot(kt[lag], rhs, preferred_element_type=F32)
            adj[2 * c] += out[:, :COLS]
            adj[2 * c + 1] += out[:, COLS:]
            return carry

        lax.fori_loop(low, high, per_lag, 0)

    def out_copy(t):
        return pltpu.make_async_copy(adj.at[t], adj_hbm.at[t], out_sem.at[t])

    def finish(c):
        for t in (2 * c, 2 * c + 1):
            edge_out[t, 0] = adj[t, 0 : 2 * COLS, :].astype(BF16)
            edge_out[t, 1] = adj[t, points - 2 * COLS : points, :].astype(BF16)
            send_halos(t, edge_copy)
            out_copy(t).start()

    last = chunks - 1
    for c in range(chunks):
        forward(c)
        if c >= 1:
            to_plane(c - 1)
        if c >= 2:
            to_z(c - 2)
        if c >= 3:
            to_gather(c - 3)
    to_plane(last)
    to_z(last - 1)
    to_gather(last - 2)
    to_twin(last - 3)
    lax.fori_loop(0, steps // 2, flip, 0)
    to_z(last)
    to_gather(last - 1)
    to_twin(last - 2)
    lax.fori_loop(steps // 2, steps, flip, 0)
    to_gather(last)
    to_twin(last - 1)
    for c in range(last):
        twin_copy(c).wait()
    early = steps - 2
    for c in range(last):
        back(c, 0, early - 2 * c - 1)
    to_twin(last)
    twin_copy(last).wait()
    for c in range(chunks):
        back(c, max(0, early - 2 * c - 1), steps - 2 * c)
        finish(c)
    for copy in coef_out:
        copy.wait()
    for t in range(steps):
        out_copy(t).wait()
        wait_halos(t, edge_copy)


def last_kernel(tiles, adj_ref, edge_ref, coef_ref, out_ref, coupled, again, swept):
    rows = out_ref.shape[2]
    tile = lax.axis_index("tile")

    @pl.when(pl.program_id(0) == 0)
    def _():
        clear_pads(coupled, rows + 4)
        clear_pads(again, rows + 2)

    def value(j):
        if j < 2:
            block = edge_ref[0, 0, j * COLS : (j + 1) * COLS, :].astype(F32)
            return jnp.where(tile > 0, block, 0.0)
        if j < rows + 2:
            return adj_ref[0, (j - 2) * COLS : (j - 1) * COLS, :]
        j = j - rows - 2
        block = edge_ref[0, 1, j * COLS : (j + 1) * COLS, :].astype(F32)
        return jnp.where(tile < tiles - 1, block, 0.0)

    def put(r, field):
        out_ref[0, 0, r] = field

    two_sweeps(
        rows, value, coef_ref.at[0 : rows + 4], coef_ref.at[rows + 4 : 2 * rows + 6], coupled, again, swept, put
    )


def split(mesh):
    bands, tiles = mesh.shape["band"], mesh.shape["tile"]
    if tiles == 64:
        return (bands // 2, 2, 4, 8)
    return (bands // 2, 1, tiles // 2, 2)


def body(sizes, sketch, diag_coef, couple, kernel, noise_prec):
    steps, _, rows, cols, width = sketch.shape
    sensors = kernel.shape[1]
    points = rows * cols
    nyl, nyh, nx, nz = sizes
    plane = nyl * nyh * nx
    tiles = nyh * nx * nz
    half = sensors // 2
    piece = half // plane
    chunks = steps // 2
    by_row = jnp.transpose(kernel, (0, 2, 3, 1, 4))
    diag_rows = jnp.transpose(diag_coef, (1, 0, 2))
    couple_rows = jnp.transpose(couple, (1, 0, 2))
    anywhere = pl.BlockSpec(memory_space=pl.ANY)
    near = pl.BlockSpec(memory_space=pltpu.VMEM)
    dma = pltpu.SemaphoreType.DMA
    sweep_scratch = [
        pltpu.VMEM((rows + 4, cols + 2 * PAD, width), F32),
        pltpu.VMEM((rows + 2, cols + 2 * PAD, width), F32),
        pltpu.VMEM((rows + 2, cols, width), F32),
    ]
    edge_shape = (steps, 2, 2 * cols, width)
    adj, edge, coef = pl.pallas_call(
        functools.partial(main_kernel, sizes),
        out_shape=(
            jax.ShapeDtypeStruct((steps, points, width), F32),
            jax.ShapeDtypeStruct(edge_shape, BF16),
            jax.ShapeDtypeStruct((2 * rows + 6, cols, width), F32),
        ),
        in_specs=[anywhere, near, near, anywhere, near],
        out_specs=(anywhere, anywhere, anywhere),
        scratch_shapes=[
            pltpu.VMEM((steps, rows, sensors, cols), BF16),
            pltpu.VMEM((steps, points, sensors), BF16),
            pltpu.VMEM((steps, rows, cols, width), F32),
            pltpu.VMEM(edge_shape, BF16),
            pltpu.VMEM(edge_shape, BF16),
            pltpu.VMEM((steps + 1, points, width), BF16),
            pltpu.VMEM((chunks, sensors, 2 * width), F32),
            pltpu.VMEM((chunks, half, 2 * width), F32),
            pltpu.VMEM((chunks, half, 2 * width), BF16),
            pltpu.VMEM((chunks, (plane - 1) * piece, 2 * width), BF16),
            pltpu.VMEM((chunks, piece, 2 * width), BF16),
            pltpu.VMEM((chunks, nz, piece, 2 * width), BF16),
            pltpu.VMEM((chunks, 2, piece, width), BF16),
            pltpu.VMEM((steps + 1, sensors, width), BF16),
            pltpu.VMEM((steps, points, width), F32),
            pltpu.VMEM(edge_shape, BF16),
            pltpu.VMEM((2, 2, rows, 1, cols), F32),
            pltpu.VMEM((rows + 4, cols, width), F32),
            pltpu.VMEM((rows + 2, cols, width), F32),
            *sweep_scratch,
            dma((2 * steps,)),
            dma((2, 2)), dma((2, 2)),
            dma((steps, 2)), dma((steps, 2)),
            dma((chunks,)), dma((chunks,)),
            dma((chunks,)), dma((chunks,)),
            dma((chunks, nz)), dma((chunks, nz)),
            dma((chunks,)), dma((chunks,)),
            dma((chunks,)), dma((chunks,)),
            dma((steps, 2)), dma((steps, 2)),
            dma((steps + 2,)),
        ],
        compiler_params=pltpu.CompilerParams(
            collective_id=0, has_side_effects=True, vmem_limit_bytes=56 * 1024 * 1024
        ),
        name="sketch_main",
    )(sketch, diag_rows, couple_rows, by_row, noise_prec)
    return pl.pallas_call(
        functools.partial(last_kernel, tiles),
        out_shape=jax.ShapeDtypeStruct(sketch.shape, F32),
        grid=(steps,),
        in_specs=[
            pl.BlockSpec((1, points, width), lambda t: (t, 0, 0)),
            pl.BlockSpec((1, 2, 2 * cols, width), lambda t: (t, 0, 0, 0)),
            pl.BlockSpec((2 * rows + 6, cols, width), lambda t: (0, 0, 0)),
        ],
        out_specs=pl.BlockSpec((1, 1, rows, cols, width), lambda t: (t, 0, 0, 0, 0)),
        scratch_shapes=sweep_scratch,
        compiler_params=pltpu.CompilerParams(vmem_limit_bytes=32 * 1024 * 1024),
        name="last_sweeps",
    )(adj, edge, coef)


def solution(mesh):
    placed = (
        P(None, "band", "tile", None, None),
        P("band", "tile", None),
        P("band", "tile", None),
        P(None, None, "band", "tile", None),
        P(),
    )
    return jax.shard_map(
        functools.partial(body, split(mesh)),
        mesh=mesh,
        in_specs=placed,
        out_specs=P(None, "band", "tile", None, None),
        check_vma=False,
    )
```

```python
import functools

import jax
import jax.numpy as jnp
from jax import lax
from jax.experimental import pallas as pl
from jax.experimental.pallas import tpu as pltpu
from jax.sharding import PartitionSpec as P

F32 = jnp.float32
BF16 = jnp.bfloat16
MESH = pl.DeviceIdType.MESH
COLS = 128
PAD = 8


def beside(ref, row):
    return ref[row, pl.ds(PAD - 1, COLS), :] + ref[row, pl.ds(PAD + 1, COLS), :]


def clear_pads(ref, rows):
    zero = jnp.zeros((PAD, ref.shape[2]), F32)
    for row in range(rows):
        ref[row, 0:PAD, :] = zero
        ref[row, PAD + COLS : 2 * PAD + COLS, :] = zero


def two_sweeps(rows, value, cpl, dia, coupled, again, swept, put):
    body = pl.ds(PAD, COLS)
    for j in range(rows + 4):
        coupled[j, body, :] = cpl[j] * value(j)
    for j in range(1, rows + 3):
        near = coupled[j - 1, body, :] + coupled[j + 1, body, :] + beside(coupled, j)
        once = dia[j - 1] * value(j) - cpl[j] * near
        swept[j - 1] = once
        again[j - 1, body, :] = cpl[j] * once
    for r in range(rows):
        q = r + 1
        near = again[q - 1, body, :] + again[q + 1, body, :] + beside(again, q)
        put(r, dia[q] * swept[q] - cpl[q + 1] * near)


class Place:
    def __init__(self, sizes):
        self.nyl, self.nyh, self.nx, self.nz = sizes
        self.tiles = self.nyh * self.nx * self.nz
        self.band = lax.axis_index("band")
        self.tile = lax.axis_index("tile")
        self.core = lax.rem(self.band, 2)
        self.z = lax.rem(self.tile, self.nz)
        self.plane = self.nyl * self.nyh * self.nx
        self.g = self.band // 2 * (self.nyh * self.nx) + self.tile // self.nz

    def twin(self):
        return (self.band + 1 - 2 * self.core, self.tile)

    def in_plane(self, d):
        g = lax.rem(self.g + d, self.plane)
        inner = self.nyh * self.nx
        return g, (g // inner * 2 + self.core, lax.rem(g, inner) * self.nz + self.z)

    def along_z(self, d):
        z = lax.rem(self.z + d, self.nz)
        return (self.band, self.tile - self.z + z)

    def row_neighbour(self, step):
        return (self.band, lax.rem(self.tile + step + self.tiles, self.tiles))


def remote(src, dst, send, recv, where):
    return pltpu.make_async_remote_copy(
        src_ref=src, dst_ref=dst, send_sem=send, recv_sem=recv, device_id=where, device_id_type=MESH
    )


def main_kernel(
    sizes,
    sketch_hbm, diag_ref, couple_ref, kern_hbm, prec_ref,
    out_hbm,
    kv, kt, sk, field, stage, hin, smooth, total, pair_in, xsend, xin, zsend, zin, wsend, wgt, adj,
    edge_out, edge_in, coef_in, cpl, dia, coupled, again, swept,
    load_sem, coef_send, coef_recv, halo_send, halo_recv, pair_send, pair_recv, x_send, x_recv,
    z_send, z_recv, g_send, g_recv, p_send, p_recv, edge_send, edge_recv, out_sem,
):
    here = Place(sizes)
    steps, rows, sensors, _ = kv.shape
    points = rows * COLS
    chunks = steps // 2
    pairs = steps // 2
    half = sensors // 2
    piece = half // here.plane
    others = here.plane - 1
    zothers = here.nz - 1
    up, down = here.row_neighbour(-1), here.row_neighbour(1)
    has_up, has_down = here.tile > 0, here.tile < here.tiles - 1
    twin = here.twin()

    sketch_loads = [
        pltpu.make_async_copy(sketch_hbm.at[t, 0], sk.at[t], load_sem.at[t]) for t in range(steps)
    ]
    kern_loads = [
        pltpu.make_async_copy(kern_hbm.at[lag, 0], kv.at[lag], load_sem.at[steps + lag])
        for lag in range(steps)
    ]
    for load in sketch_loads:
        load.start()
    for load in kern_loads:
        load.start()

    barrier = pltpu.get_barrier_semaphore()
    greeted = [up, down, twin]
    greeted += [here.in_plane(d)[1] for d in range(1, here.plane)]
    greeted += [here.along_z(d) for d in range(1, here.nz)]
    for where in greeted:
        pl.semaphore_signal(barrier, inc=1, device_id=where, device_id_type=MESH)

    low = lax.broadcasted_iota(jnp.int32, (COLS, COLS), 1) < COLS // 2

    def turn(x):
        return pltpu.roll(x, COLS // 2, 1)

    clear_pads(coupled, rows + 4)
    clear_pads(again, rows + 2)
    for h in range(2):
        smooth[h, 0, 0] = jnp.zeros((points, COLS), BF16)
        smooth[h, 1, 0] = jnp.zeros((points, COLS), BF16)
        wgt[h, 0, pairs] = jnp.zeros((sensors, COLS), BF16)
        wgt[h, 1, pairs + 1] = jnp.zeros((sensors, COLS), BF16)

    @pl.when(jnp.logical_not(has_up))
    def _():
        hin[:, 0] = jnp.zeros((steps, 2 * COLS, COLS), BF16)
        edge_in[:, 0] = jnp.zeros((steps, 2 * COLS, COLS), BF16)

    @pl.when(jnp.logical_not(has_down))
    def _():
        hin[:, 1] = jnp.zeros((steps, 2 * COLS, COLS), BF16)
        edge_in[:, 1] = jnp.zeros((steps, 2 * COLS, COLS), BF16)

    for p in range(pairs):
        sketch_loads[2 * p].wait()
        sketch_loads[2 * p + 1].wait()

        def pack(r, carry, p=p):
            first, second = sk[2 * p, r], sk[2 * p + 1, r]
            field[p, r] = jnp.where(low, first, turn(second))
            field[pairs + p, r] = jnp.where(low, turn(first), second)
            return carry

        lax.fori_loop(0, rows, pack, 0)
        for f in (p, pairs + p):
            stage[f, 0] = field[f, 0:2].reshape(2 * COLS, COLS).astype(BF16)
            stage[f, 1] = field[f, rows - 2 : rows].reshape(2 * COLS, COLS).astype(BF16)

    pl.semaphore_wait(barrier, len(greeted))

    def coef_copies(side, where):
        return [
            remote(ref, coef_in.at[side, i], coef_send.at[side, i], coef_recv.at[side, i], where)
            for i, ref in enumerate((couple_ref, diag_ref))
        ]

    def halo_copy(f, side, where):
        return remote(
            stage.at[f, 1 - side], hin.at[f, side], halo_send.at[f, side], halo_recv.at[f, side], where
        )

    def edge_copy(f, side, where):
        return remote(
            edge_out.at[f, 1 - side], edge_in.at[f, side], edge_send.at[f, side], edge_recv.at[f, side], where
        )

    def send_halos(f, copy):
        @pl.when(has_up)
        def _():
            copy(f, 1, up).start()

        @pl.when(has_down)
        def _():
            copy(f, 0, down).start()

    def wait_halos(f, copy):
        @pl.when(has_up)
        def _():
            copy(f, 0, up).wait_recv()
            copy(f, 1, up).wait_send()

        @pl.when(has_down)
        def _():
            copy(f, 1, down).wait_recv()
            copy(f, 0, down).wait_send()

    @pl.when(has_up)
    def _():
        for copy in coef_copies(1, up):
            copy.start()

    @pl.when(has_down)
    def _():
        for copy in coef_copies(0, down):
            copy.start()

    for f in range(steps):
        send_halos(f, halo_copy)

    def over_lanes(row):
        return jnp.broadcast_to(row, (COLS, COLS)).T

    for r in range(rows):
        cpl[r + 2] = over_lanes(couple_ref[r])
        dia[r + 1] = over_lanes(diag_ref[r])

    blank = jnp.zeros((COLS, COLS), F32)

    @pl.when(jnp.logical_not(has_up))
    def _():
        cpl[0] = blank
        cpl[1] = blank
        dia[0] = blank

    @pl.when(jnp.logical_not(has_down))
    def _():
        cpl[rows + 2] = blank
        cpl[rows + 3] = blank
        dia[rows + 1] = blank

    def flip(lag, carry):
        for r in range(rows):
            kt[lag, r * COLS : (r + 1) * COLS, :] = kv[lag, r].T
        return carry

    for load in kern_loads:
        load.wait()
    lax.fori_loop(0, steps // 2, flip, 0)

    @pl.when(has_up)
    def _():
        for copy in coef_copies(0, up):
            copy.wait_recv()
        for copy in coef_copies(1, up):
            copy.wait_send()
        cpl[0] = over_lanes(coef_in[0, 0, rows - 2])
        cpl[1] = over_lanes(coef_in[0, 0, rows - 1])
        dia[0] = over_lanes(coef_in[0, 1, rows - 1])

    @pl.when(has_down)
    def _():
        for copy in coef_copies(1, down):
            copy.wait_recv()
        for copy in coef_copies(0, down):
            copy.wait_send()
        cpl[rows + 2] = over_lanes(coef_in[1, 0, 0])
        cpl[rows + 3] = over_lanes(coef_in[1, 0, 1])
        dia[rows + 1] = over_lanes(coef_in[1, 1, 0])

    my_half = pl.multiple_of(here.core * half, half)
    twin_half = pl.multiple_of(half - here.core * half, half)
    my_piece = pl.multiple_of(here.g * piece, piece)
    my_sensors = pl.multiple_of(here.core * half + here.g * piece, piece)

    def rows_of(own, edges, f):
        def value(j):
            if j < 2:
                return edges[f, 0, j * COLS : (j + 1) * COLS, :].astype(F32)
            if j < rows + 2:
                return own(j - 2)
            j = j - rows - 2
            return edges[f, 1, j * COLS : (j + 1) * COLS, :].astype(F32)

        return value

    def sweeps(value, put):
        two_sweeps(rows, value, cpl, dia, coupled, again, swept, put)

    def smooth_field(h, f):
        p = f - h * pairs
        wait_halos(f, halo_copy)

        def put(r, new):
            block = slice(r * COLS, (r + 1) * COLS)
            before = smooth[h, 0, p, block, :].astype(F32)
            smooth[h, 0, p + 1, block, :] = new.astype(BF16)
            smooth[h, 1, p + 1, block, :] = turn(jnp.where(low, new, before)).astype(BF16)

        sweeps(rows_of(lambda r: field[f, r], hin, f), put)

    def pair_copy(c):
        return remote(
            total.at[c, pl.ds(twin_half, half)], pair_in.at[c], pair_send.at[c], pair_recv.at[c], twin
        )

    def forward(c):
        h, q = c // 2, c % 2
        total[c] = jnp.zeros((sensors, 2 * COLS), F32)

        def per_lag(lag, carry):
            odd, at = lax.rem(lag, 2), 2 * q + 1 - lax.div(lag, 2)
            lhs = jnp.concatenate([kv[lag, r] for r in range(rows)], axis=1)
            rhs = jnp.concatenate([smooth[h, odd, at], smooth[h, odd, at + 1]], axis=1)
            total[c] += jnp.dot(lhs, rhs, preferred_element_type=F32)
            return carry

        if q:
            lax.fori_loop(4, 8, per_lag, 0)

        def per_field(f, carry):
            smooth_field(h, f)
            return carry

        lax.fori_loop(2 * c, 2 * c + 2, per_field, 0)
        lax.fori_loop(0, 4, per_lag, 0)
        pair_copy(c).start()

    def plane_copies(c):
        copies = []
        for d in range(1, here.plane):
            g, where = here.in_plane(d)
            copies.append(
                remote(
                    xsend.at[c, pl.ds(pl.multiple_of(g * piece, piece), piece)],
                    xin.at[c, pl.ds((d - 1) * piece, piece)],
                    x_send.at[c], x_recv.at[c], where,
                )
            )
        return copies

    def bulk(c, send, recv):
        block = xin.at[c]
        return remote(block, block, send, recv, twin)

    def to_plane(c):
        pair_copy(c).wait()
        xsend[c] = (total[c, pl.ds(my_half, half)] + pair_in[c]).astype(BF16)
        for copy in plane_copies(c):
            copy.start()

    def z_copies(c):
        return [
            remote(zsend.at[c], zin.at[c, d - 1], z_send.at[c, d], z_recv.at[c, d], here.along_z(d))
            for d in range(1, here.nz)
        ]

    def own_sum(c):
        rows_here = pl.ds(pl.multiple_of(my_half + my_piece, piece), piece)
        acc = total[c, rows_here] + pair_in[c, pl.ds(my_piece, piece)]
        for d in range(others):
            acc = acc + xin[c, d * piece : (d + 1) * piece].astype(F32)
        return acc

    def to_z(c):
        bulk(c, x_send.at[c], x_recv.at[c]).wait()
        zsend[c] = own_sum(c).astype(BF16)
        for copy in z_copies(c):
            copy.start()

    def gather_copies(c):
        h, q = c // 2, c % 2
        return [
            remote(
                wsend.at[c],
                wgt.at[h, 0, pl.ds(2 * q, 2), pl.ds(my_sensors, piece)],
                g_send.at[c], g_recv.at[c], here.in_plane(d)[1],
            )
            for d in range(1, here.plane)
        ]

    spot = lax.broadcasted_iota(jnp.int32, (piece, sensors), 1)
    wanted = lax.broadcasted_iota(jnp.int32, (piece, sensors), 0) + my_sensors
    left = lax.broadcasted_iota(jnp.int32, (piece, COLS), 1) < COLS // 2

    def scale_of(t):
        return jnp.sum(jnp.where(spot == wanted, prec_ref[t : t + 1, :], 0.0), axis=1, keepdims=True)

    def to_gather(c):
        h, q = c // 2, c % 2
        for copy in z_copies(c):
            copy.wait()
        acc = own_sum(c)
        for d in range(zothers):
            acc = acc + zin[c, d].astype(F32)
        for i in range(2):
            t = 4 * q + 2 * i
            scale = jnp.where(left, scale_of(t), scale_of(t + 1))
            block = (acc[:, i * COLS : (i + 1) * COLS] * scale).astype(BF16)
            wsend[c, i] = block
            wgt[h, 0, 2 * q + i, pl.ds(my_sensors, piece), :] = block
        for copy in gather_copies(c):
            copy.start()

    def twin_copy(c):
        h, q = c // 2, c % 2
        block = wgt.at[h, 0, pl.ds(2 * q, 2), pl.ds(my_half, half)]
        return remote(block, block, p_send.at[c], p_recv.at[c], twin)

    def to_twin(c):
        bulk(c, g_send.at[c], g_recv.at[c]).wait()
        twin_copy(c).start()

    def weights_in(c):
        h, q = c // 2, c % 2
        twin_copy(c).wait()
        for p in (2, 3, 4) if q else (1,):
            for s in range(0, sensors, COLS):
                block = slice(s, s + COLS)
                mixed = jnp.where(low, wgt[h, 0, p, block, :].astype(F32), wgt[h, 0, p - 1, block, :].astype(F32))
                wgt[h, 1, p, block, :] = turn(mixed).astype(BF16)

    def back(c):
        h, q = c // 2, c % 2
        adj[2 * c] = jnp.zeros((points, COLS), F32)
        adj[2 * c + 1] = jnp.zeros((points, COLS), F32)

        def per_lag(lag, carry):
            odd, at = lax.rem(lag, 2), 2 * q + lax.div(lag + 1, 2)
            rhs = jnp.concatenate([wgt[h, odd, at], wgt[h, odd, at + 1]], axis=1)
            out = jnp.dot(kt[lag], rhs, preferred_element_type=F32)
            adj[2 * c] += out[:, :COLS]
            adj[2 * c + 1] += out[:, COLS:]
            return carry

        lax.fori_loop(0, steps - 4 * q, per_lag, 0)
        for f in (2 * c, 2 * c + 1):
            edge_out[f, 0] = adj[f, 0 : 2 * COLS, :].astype(BF16)
            edge_out[f, 1] = adj[f, points - 2 * COLS : points, :].astype(BF16)
            send_halos(f, edge_copy)

    def out_copy(t):
        return pltpu.make_async_copy(sk.at[t], out_hbm.at[t, 0], out_sem.at[t])

    def result(f):
        wait_halos(f, edge_copy)
        return rows_of(lambda r: adj[f, pl.ds(r * COLS, COLS), :], edge_in, f)

    def first_half(p, carry):
        def put(r, new):
            field[p, r] = new

        sweeps(result(p), put)
        return carry

    def second_half(p, carry):
        def put(r, new):
            before = field[p, r]
            sk[2 * p, r] = jnp.where(low, before, turn(new))
            sk[2 * p + 1, r] = jnp.where(low, turn(before), new)

        sweeps(result(pairs + p), put)
        out_copy(2 * p).start()
        out_copy(2 * p + 1).start()
        return carry

    forward(0)
    forward(1)
    to_plane(0)
    forward(2)
    to_plane(1)
    to_z(0)
    forward(3)
    to_plane(2)
    to_z(1)
    to_plane(3)
    to_gather(0)
    lax.fori_loop(steps // 2, steps, flip, 0)
    to_z(2)
    to_gather(1)
    to_z(3)
    to_twin(0)
    to_gather(2)
    to_twin(1)
    to_gather(3)
    weights_in(0)
    weights_in(1)
    back(1)
    back(0)
    to_twin(2)
    to_twin(3)
    weights_in(2)
    weights_in(3)
    back(3)
    back(2)
    lax.fori_loop(2, 4, first_half, 0)
    lax.fori_loop(0, 2, first_half, 0)
    lax.fori_loop(2, 4, second_half, 0)
    lax.fori_loop(0, 2, second_half, 0)
    for t in range(steps):
        out_copy(t).wait()


def split(mesh):
    bands, tiles = mesh.shape["band"], mesh.shape["tile"]
    if tiles == 64:
        return (bands // 2, 2, 4, 8)
    return (bands // 2, 1, tiles // 2, 2)


def body(sizes, sketch, diag_coef, couple, kernel, noise_prec):
    steps, _, rows, cols, width = sketch.shape
    sensors = kernel.shape[1]
    points = rows * cols
    nyl, nyh, nx, nz = sizes
    plane = nyl * nyh * nx
    tiles = nyh * nx * nz
    half = sensors // 2
    piece = half // plane
    chunks = steps // 2
    by_row = jnp.transpose(kernel, (0, 2, 3, 1, 4))
    diag_rows = jnp.transpose(diag_coef, (1, 0, 2))
    couple_rows = jnp.transpose(couple, (1, 0, 2))
    anywhere = pl.BlockSpec(memory_space=pl.ANY)
    near = pl.BlockSpec(memory_space=pltpu.VMEM)
    dma = pltpu.SemaphoreType.DMA
    sweep_scratch = [
        pltpu.VMEM((rows + 4, cols + 2 * PAD, width), F32),
        pltpu.VMEM((rows + 2, cols + 2 * PAD, width), F32),
        pltpu.VMEM((rows + 2, cols, width), F32),
    ]
    edge_shape = (steps, 2, 2 * cols, width)
    return pl.pallas_call(
        functools.partial(main_kernel, sizes),
        out_shape=jax.ShapeDtypeStruct(sketch.shape, F32),
        in_specs=[anywhere, near, near, anywhere, near],
        out_specs=anywhere,
        scratch_shapes=[
            pltpu.VMEM((steps, rows, sensors, cols), BF16),
            pltpu.VMEM((steps, points, sensors), BF16),
            pltpu.VMEM((steps, rows, cols, width), F32),
            pltpu.VMEM((steps, rows, cols, width), F32),
            pltpu.VMEM(edge_shape, BF16),
            pltpu.VMEM(edge_shape, BF16),
            pltpu.VMEM((2, 2, chunks + 1, points, width), BF16),
            pltpu.VMEM((chunks, sensors, 2 * width), F32),
            pltpu.VMEM((chunks, half, 2 * width), F32),
            pltpu.VMEM((chunks, half, 2 * width), BF16),
            pltpu.VMEM((chunks, (plane - 1) * piece, 2 * width), BF16),
            pltpu.VMEM((chunks, piece, 2 * width), BF16),
            pltpu.VMEM((chunks, nz - 1, piece, 2 * width), BF16),
            pltpu.VMEM((chunks, 2, piece, width), BF16),
            pltpu.VMEM((2, 2, chunks + 2, sensors, width), BF16),
            pltpu.VMEM((steps, points, width), F32),
            pltpu.VMEM(edge_shape, BF16),
            pltpu.VMEM(edge_shape, BF16),
            pltpu.VMEM((2, 2, rows, 1, cols), F32),
            pltpu.VMEM((rows + 4, cols, width), F32),
            pltpu.VMEM((rows + 2, cols, width), F32),
            *sweep_scratch,
            dma((2 * steps,)),
            dma((2, 2)), dma((2, 2)),
            dma((steps, 2)), dma((steps, 2)),
            dma((chunks,)), dma((chunks,)),
            dma((chunks,)), dma((chunks,)),
            dma((chunks, nz)), dma((chunks, nz)),
            dma((chunks,)), dma((chunks,)),
            dma((chunks,)), dma((chunks,)),
            dma((steps, 2)), dma((steps, 2)),
            dma((steps,)),
        ],
        compiler_params=pltpu.CompilerParams(
            collective_id=0, has_side_effects=True, vmem_limit_bytes=60 * 1024 * 1024
        ),
        name="sketch_main",
    )(sketch, diag_rows, couple_rows, by_row, noise_prec)


def solution(mesh):
    placed = (
        P(None, "band", "tile", None, None),
        P("band", "tile", None),
        P("band", "tile", None),
        P(None, None, "band", "tile", None),
        P(),
    )
    return jax.shard_map(
        functools.partial(body, split(mesh)),
        mesh=mesh,
        in_specs=placed,
        out_specs=P(None, "band", "tile", None, None),
        check_vma=False,
    )
```

```python
import functools

import jax
import jax.numpy as jnp
from jax import lax
from jax.experimental import pallas as pl
from jax.experimental.pallas import tpu as pltpu
from jax.sharding import PartitionSpec as P

F32 = jnp.float32
BF16 = jnp.bfloat16
MESH = pl.DeviceIdType.MESH
COLS = 128
PAD = 8


def beside(ref, row):
    return ref[row, pl.ds(PAD - 1, COLS), :] + ref[row, pl.ds(PAD + 1, COLS), :]


def clear_pads(ref, rows):
    zero = jnp.zeros((PAD, ref.shape[2]), F32)
    for row in range(rows):
        ref[row, 0:PAD, :] = zero
        ref[row, PAD + COLS : 2 * PAD + COLS, :] = zero


def two_sweeps(rows, value, cpl, dia, coupled, again, swept, put):
    body = pl.ds(PAD, COLS)
    for j in range(rows + 4):
        coupled[j, body, :] = cpl[j] * value(j)
    for j in range(1, rows + 3):
        near = coupled[j - 1, body, :] + coupled[j + 1, body, :] + beside(coupled, j)
        once = dia[j - 1] * value(j) - cpl[j] * near
        swept[j - 1] = once
        again[j - 1, body, :] = cpl[j] * once
    for r in range(rows):
        q = r + 1
        near = again[q - 1, body, :] + again[q + 1, body, :] + beside(again, q)
        put(r, dia[q] * swept[q] - cpl[q + 1] * near)


class Place:
    def __init__(self, sizes):
        self.nyl, self.nyh, self.nx, self.nz = sizes
        self.tiles = self.nyh * self.nx * self.nz
        self.band = lax.axis_index("band")
        self.tile = lax.axis_index("tile")
        self.core = lax.rem(self.band, 2)
        self.z = lax.rem(self.tile, self.nz)
        self.plane = self.nyl * self.nyh * self.nx
        self.g = self.band // 2 * (self.nyh * self.nx) + self.tile // self.nz

    def twin(self):
        return (self.band + 1 - 2 * self.core, self.tile)

    def in_plane(self, d):
        g = lax.rem(self.g + d, self.plane)
        inner = self.nyh * self.nx
        return g, (g // inner * 2 + self.core, lax.rem(g, inner) * self.nz + self.z)

    def along_z(self, d):
        z = lax.rem(self.z + d, self.nz)
        return (self.band, self.tile - self.z + z)

    def row_neighbour(self, step):
        return (self.band, lax.rem(self.tile + step + self.tiles, self.tiles))


def remote(src, dst, send, recv, where):
    return pltpu.make_async_remote_copy(
        src_ref=src, dst_ref=dst, send_sem=send, recv_sem=recv, device_id=where, device_id_type=MESH
    )


def main_kernel(
    sizes,
    sketch_hbm, diag_hbm, couple_hbm, kern_hbm, prec_hbm,
    out_hbm,
    diag_ref, couple_ref, prec_ref,
    kv, kt, sk, field, stage, hin, smooth, total, pair_in, xsend, xin, zsend, zin, wsend, wgt, adj,
    edge_out, edge_in, coef_in, cpl, dia, coupled, again, swept,
    load_sem, coef_send, coef_recv, halo_send, halo_recv, pair_send, pair_recv, x_send, x_recv,
    z_send, z_recv, g_send, g_recv, p_send, p_recv, edge_send, edge_recv, out_sem,
):
    here = Place(sizes)
    steps, rows, sensors, _ = kv.shape
    points = rows * COLS
    chunks = steps // 2
    pairs = steps // 2
    half = sensors // 2
    piece = half // here.plane
    others = here.plane - 1
    zothers = here.nz - 1
    up, down = here.row_neighbour(-1), here.row_neighbour(1)
    has_up, has_down = here.tile > 0, here.tile < here.tiles - 1
    twin = here.twin()

    sketch_loads = [
        pltpu.make_async_copy(sketch_hbm.at[t, 0], sk.at[t], load_sem.at[t]) for t in range(steps)
    ]
    kern_loads = [
        pltpu.make_async_copy(kern_hbm.at[lag, 0], kv.at[lag], load_sem.at[steps + lag])
        for lag in range(steps)
    ]
    small_loads = [
        pltpu.make_async_copy(src, dst, load_sem.at[2 * steps + i])
        for i, (src, dst) in enumerate(
            ((couple_hbm, couple_ref), (diag_hbm, diag_ref), (prec_hbm, prec_ref))
        )
    ]
    barrier = pltpu.get_barrier_semaphore()
    greeted = [up, down, twin]
    greeted += [here.in_plane(d)[1] for d in range(1, here.plane)]
    greeted += [here.along_z(d) for d in range(1, here.nz)]
    for load in sketch_loads:
        load.start()
    for where in greeted:
        pl.semaphore_signal(barrier, inc=1, device_id=where, device_id_type=MESH)
    for load in small_loads + kern_loads:
        load.start()

    low = lax.broadcasted_iota(jnp.int32, (COLS, COLS), 1) < COLS // 2

    def turn(x):
        return pltpu.roll(x, COLS // 2, 1)

    def coef_copies(side, where):
        return [
            remote(ref, coef_in.at[side, i], coef_send.at[side, i], coef_recv.at[side, i], where)
            for i, ref in enumerate((couple_hbm, diag_hbm))
        ]

    def halo_copy(f, side, where):
        return remote(
            stage.at[f, 1 - side], hin.at[f, side], halo_send.at[f, side], halo_recv.at[f, side], where
        )

    def edge_copy(f, side, where):
        return remote(
            edge_out.at[f, 1 - side], edge_in.at[f, side], edge_send.at[f, side], edge_recv.at[f, side], where
        )

    def send_halos(f, copy):
        @pl.when(has_up)
        def _():
            copy(f, 1, up).start()

        @pl.when(has_down)
        def _():
            copy(f, 0, down).start()

    def wait_halos(f, copy):
        @pl.when(has_up)
        def _():
            copy(f, 0, up).wait_recv()
            copy(f, 1, up).wait_send()

        @pl.when(has_down)
        def _():
            copy(f, 1, down).wait_recv()
            copy(f, 0, down).wait_send()

    for p in range(pairs):
        sketch_loads[2 * p].wait()
        sketch_loads[2 * p + 1].wait()

        for r in range(rows):
            first, second = sk[2 * p, r], sk[2 * p + 1, r]
            crossed = turn(jnp.where(low, second, first))
            field[p, r] = jnp.where(low, first, crossed)
            field[pairs + p, r] = jnp.where(low, crossed, second)
        for f in (p, pairs + p):
            stage[f, 0] = field[f, 0:2].reshape(2 * COLS, COLS).astype(BF16)
            stage[f, 1] = field[f, rows - 2 : rows].reshape(2 * COLS, COLS).astype(BF16)
        if p == 0:
            pl.semaphore_wait(barrier, len(greeted))

            @pl.when(has_up)
            def _():
                for copy in coef_copies(1, up):
                    copy.start()

            @pl.when(has_down)
            def _():
                for copy in coef_copies(0, down):
                    copy.start()

        send_halos(p, halo_copy)
    for p in range(pairs):
        send_halos(pairs + p, halo_copy)

    clear_pads(coupled, rows + 4)
    clear_pads(again, rows + 2)
    total[...] = jnp.zeros(total.shape, F32)
    adj[...] = jnp.zeros(adj.shape, F32)
    for h in range(2):
        smooth[h, 0, 0] = jnp.zeros((points, COLS), BF16)
        smooth[h, 1, 0] = jnp.zeros((points, COLS), BF16)
        wgt[h, 0, pairs] = jnp.zeros((sensors, COLS), BF16)
        wgt[h, 1, pairs + 1] = jnp.zeros((sensors, COLS), BF16)

    @pl.when(jnp.logical_not(has_up))
    def _():
        hin[:, 0] = jnp.zeros((steps, 2 * COLS, COLS), BF16)
        edge_in[:, 0] = jnp.zeros((steps, 2 * COLS, COLS), BF16)

    @pl.when(jnp.logical_not(has_down))
    def _():
        hin[:, 1] = jnp.zeros((steps, 2 * COLS, COLS), BF16)
        edge_in[:, 1] = jnp.zeros((steps, 2 * COLS, COLS), BF16)

    for load in small_loads:
        load.wait()

    def over_lanes(row):
        return jnp.broadcast_to(row, (COLS, COLS)).T

    for r in range(rows):
        cpl[r + 2] = over_lanes(couple_ref[r])
        dia[r + 1] = over_lanes(diag_ref[r])

    blank = jnp.zeros((COLS, COLS), F32)

    @pl.when(jnp.logical_not(has_up))
    def _():
        cpl[0] = blank
        cpl[1] = blank
        dia[0] = blank

    @pl.when(jnp.logical_not(has_down))
    def _():
        cpl[rows + 2] = blank
        cpl[rows + 3] = blank
        dia[rows + 1] = blank

    def flip(lag, carry):
        for r in range(rows):
            kt[lag, r * COLS : (r + 1) * COLS, :] = kv[lag, r].T
        return carry

    for lag in range(steps // 2):
        kern_loads[lag].wait()
    lax.fori_loop(0, steps // 2, flip, 0)

    @pl.when(has_up)
    def _():
        for copy in coef_copies(0, up):
            copy.wait_recv()
        for copy in coef_copies(1, up):
            copy.wait_send()
        cpl[0] = over_lanes(coef_in[0, 0, rows - 2])
        cpl[1] = over_lanes(coef_in[0, 0, rows - 1])
        dia[0] = over_lanes(coef_in[0, 1, rows - 1])

    @pl.when(has_down)
    def _():
        for copy in coef_copies(1, down):
            copy.wait_recv()
        for copy in coef_copies(0, down):
            copy.wait_send()
        cpl[rows + 2] = over_lanes(coef_in[1, 0, 0])
        cpl[rows + 3] = over_lanes(coef_in[1, 0, 1])
        dia[rows + 1] = over_lanes(coef_in[1, 1, 0])

    my_half = pl.multiple_of(here.core * half, half)
    twin_half = pl.multiple_of(half - here.core * half, half)
    my_piece = pl.multiple_of(here.g * piece, piece)
    my_sensors = pl.multiple_of(here.core * half + here.g * piece, piece)

    def rows_of(own, edges, f):
        def value(j):
            if j < 2:
                return edges[f, 0, j * COLS : (j + 1) * COLS, :].astype(F32)
            if j < rows + 2:
                return own(j - 2)
            j = j - rows - 2
            return edges[f, 1, j * COLS : (j + 1) * COLS, :].astype(F32)

        return value

    def sweeps(value, put):
        two_sweeps(rows, value, cpl, dia, coupled, again, swept, put)

    def smooth_field(h, f):
        p = f - h * pairs
        wait_halos(f, halo_copy)

        def put(r, new):
            block = slice(r * COLS, (r + 1) * COLS)
            before = smooth[h, 0, p, block, :].astype(F32)
            smooth[h, 0, p + 1, block, :] = new.astype(BF16)
            smooth[h, 1, p + 1, block, :] = turn(jnp.where(low, new, before)).astype(BF16)

        sweeps(rows_of(lambda r: field[f, r], hin, f), put)

    def pair_copy(c):
        return remote(
            total.at[c, pl.ds(twin_half, half)], pair_in.at[c], pair_send.at[c], pair_recv.at[c], twin
        )

    def lags_dot(lags, lhs, rhs):
        left_side = jnp.concatenate([x for lag in lags for x in lhs(lag)], axis=1)
        right_side = jnp.concatenate([jnp.concatenate(rhs(lag), axis=1) for lag in lags], axis=0)
        return jnp.dot(left_side, right_side, preferred_element_type=F32)

    def at_step(step, wanted, *actions):
        @pl.when(step == wanted)
        def _():
            for action in actions:
                action()

    def forward(k, carry):
        h, i = k // 3, lax.rem(k, 3)
        q = (i + 1) // 2
        c = 2 * h + q
        fresh = i != 1
        start = jnp.where(fresh, 0, 4)

        at_step(k, 1, rest_of_kernel)
        at_step(k, 2, lambda: to_plane(0))
        at_step(k, 5, lambda: to_z(0), lambda: to_plane(2))

        @pl.when(fresh)
        def _():
            def per_field(f, inner):
                smooth_field(h, f)
                return inner

            lax.fori_loop(2 * c, 2 * c + 2, per_field, 0)

        at_step(k, 3, lambda: to_plane(1))
        at_step(k, 5, lambda: to_z(1))
        first = 2 * q + 1 - start // 2

        def lhs(lag):
            return [kv[start + lag, r] for r in range(rows)]

        def rhs(lag):
            odd, at = lag % 2, first - lag // 2
            return [smooth[h, odd, at], smooth[h, odd, at + 1]]

        total[c] += lags_dot(range(4), lhs, rhs)

        @pl.when(fresh)
        def _():
            pair_copy(c).start()

        return carry

    def plane_copies(c):
        copies = []
        for d in range(1, here.plane):
            g, where = here.in_plane(d)
            copies.append(
                remote(
                    xsend.at[c, pl.ds(pl.multiple_of(g * piece, piece), piece)],
                    xin.at[c, pl.ds((d - 1) * piece, piece)],
                    x_send.at[c], x_recv.at[c], where,
                )
            )
        return copies

    def bulk(c, send, recv):
        block = xin.at[c]
        return remote(block, block, send, recv, twin)

    def to_plane(c):
        pair_copy(c).wait()
        xsend[c] = (total[c, pl.ds(my_half, half)] + pair_in[c]).astype(BF16)
        for copy in plane_copies(c):
            copy.start()

    def z_copies(c):
        return [
            remote(zsend.at[c], zin.at[c, d - 1], z_send.at[c, d], z_recv.at[c, d], here.along_z(d))
            for d in range(1, here.nz)
        ]

    def own_sum(c):
        rows_here = pl.ds(pl.multiple_of(my_half + my_piece, piece), piece)
        acc = total[c, rows_here] + pair_in[c, pl.ds(my_piece, piece)]
        for d in range(others):
            acc = acc + xin[c, d * piece : (d + 1) * piece].astype(F32)
        return acc

    def to_z(c):
        bulk(c, x_send.at[c], x_recv.at[c]).wait()
        zsend[c] = own_sum(c).astype(BF16)
        for copy in z_copies(c):
            copy.start()

    def gather_copies(c):
        h, q = c // 2, c % 2
        return [
            remote(
                wsend.at[c],
                wgt.at[h, 0, pl.ds(2 * q, 2), pl.ds(my_sensors, piece)],
                g_send.at[c], g_recv.at[c], here.in_plane(d)[1],
            )
            for d in range(1, here.plane)
        ]

    spot = lax.broadcasted_iota(jnp.int32, (piece, sensors), 1)
    wanted = lax.broadcasted_iota(jnp.int32, (piece, sensors), 0) + my_sensors
    left = lax.broadcasted_iota(jnp.int32, (piece, COLS), 1) < COLS // 2

    def scale_of(t):
        return jnp.sum(jnp.where(spot == wanted, prec_ref[t : t + 1, :], 0.0), axis=1, keepdims=True)

    def to_gather(c):
        h, q = c // 2, c % 2
        for copy in z_copies(c):
            copy.wait()
        acc = own_sum(c)
        for d in range(zothers):
            acc = acc + zin[c, d].astype(F32)
        for i in range(2):
            t = 4 * q + 2 * i
            scale = jnp.where(left, scale_of(t), scale_of(t + 1))
            block = (acc[:, i * COLS : (i + 1) * COLS] * scale).astype(BF16)
            wsend[c, i] = block
            wgt[h, 0, 2 * q + i, pl.ds(my_sensors, piece), :] = block
        for copy in gather_copies(c):
            copy.start()

    def twin_copy(c):
        h, q = c // 2, c % 2
        block = wgt.at[h, 0, pl.ds(2 * q, 2), pl.ds(my_half, half)]
        return remote(block, block, p_send.at[c], p_recv.at[c], twin)

    def to_twin(c):
        bulk(c, g_send.at[c], g_recv.at[c]).wait()
        twin_copy(c).start()

    def weights_in(c):
        h, q = c // 2, c % 2
        twin_copy(c).wait()
        for p in (2, 3, 4) if q else (1,):
            for s in range(0, sensors, COLS):
                block = slice(s, s + COLS)
                mixed = jnp.where(low, wgt[h, 0, p, block, :].astype(F32), wgt[h, 0, p - 1, block, :].astype(F32))
                wgt[h, 1, p, block, :] = turn(mixed).astype(BF16)

    def back(k, carry):
        h, i = k // 3, lax.rem(k, 3)
        q = jnp.where(i == 0, 1, 0)
        c = 2 * h + q
        start = jnp.where(i == 2, 4, 0)
        at_step(k, 3, lambda: to_twin(2), lambda: to_twin(3), lambda: weights_in(2), lambda: weights_in(3))
        first = 2 * q + start // 2

        def lhs(lag):
            return [kt[start + lag]]

        def rhs(lag):
            odd, at = lag % 2, first + (lag + 1) // 2
            return [wgt[h, odd, at], wgt[h, odd, at + 1]]

        out = lags_dot(range(4), lhs, rhs)
        adj[2 * c] += out[:, :COLS]
        adj[2 * c + 1] += out[:, COLS:]

        @pl.when(i != 1)
        def _():
            for f in (2 * c, 2 * c + 1):
                edge_out[f, 0] = adj[f, 0 : 2 * COLS, :].astype(BF16)
                edge_out[f, 1] = adj[f, points - 2 * COLS : points, :].astype(BF16)
                send_halos(f, edge_copy)

        return carry

    def out_copy(t):
        return pltpu.make_async_copy(sk.at[t], out_hbm.at[t, 0], out_sem.at[t])

    def result(f):
        wait_halos(f, edge_copy)
        return rows_of(lambda r: adj[f, pl.ds(r * COLS, COLS), :], edge_in, f)

    def first_half(k, carry):
        p = lax.rem(k + 2, pairs)

        def put(r, new):
            field[p, r] = new

        sweeps(result(p), put)
        return carry

    def second_half(k, carry):
        p = lax.rem(k + 2, pairs)

        def put(r, new):
            before = field[p, r]
            crossed = turn(jnp.where(low, new, before))
            sk[2 * p, r] = jnp.where(low, before, crossed)
            sk[2 * p + 1, r] = jnp.where(low, crossed, new)

        sweeps(result(pairs + p), put)
        out_copy(2 * p).start()
        out_copy(2 * p + 1).start()
        return carry

    def rest_of_kernel():
        for lag in range(steps // 2, steps):
            kern_loads[lag].wait()

    lax.fori_loop(0, 6, forward, 0)
    to_plane(3)
    lax.fori_loop(steps // 2, steps, flip, 0)
    to_gather(0)
    to_z(2)
    to_gather(1)
    to_z(3)
    to_twin(0)
    to_gather(2)
    to_twin(1)
    to_gather(3)
    weights_in(0)
    weights_in(1)
    lax.fori_loop(0, 6, back, 0)
    lax.fori_loop(0, pairs, first_half, 0)
    lax.fori_loop(0, pairs, second_half, 0)
    for t in range(steps):
        out_copy(t).wait()


def split(mesh):
    bands, tiles = mesh.shape["band"], mesh.shape["tile"]
    if tiles == 64:
        return (bands // 2, 2, 4, 8)
    return (bands // 2, 1, tiles // 2, 2)


def body(sizes, sketch, diag_coef, couple, kernel, noise_prec):
    steps, _, rows, cols, width = sketch.shape
    sensors = kernel.shape[1]
    points = rows * cols
    nyl, nyh, nx, nz = sizes
    plane = nyl * nyh * nx
    tiles = nyh * nx * nz
    half = sensors // 2
    piece = half // plane
    chunks = steps // 2
    by_row = jnp.transpose(kernel, (0, 2, 3, 1, 4))
    diag_rows = jnp.transpose(diag_coef, (1, 0, 2))
    couple_rows = jnp.transpose(couple, (1, 0, 2))
    anywhere = pl.BlockSpec(memory_space=pl.ANY)

    def far(x):
        return pltpu.with_memory_space_constraint(x, pltpu.HBM)

    dma = pltpu.SemaphoreType.DMA
    sweep_scratch = [
        pltpu.VMEM((rows + 4, cols + 2 * PAD, width), F32),
        pltpu.VMEM((rows + 2, cols + 2 * PAD, width), F32),
        pltpu.VMEM((rows + 2, cols, width), F32),
    ]
    edge_shape = (steps, 2, 2 * cols, width)
    return pl.pallas_call(
        functools.partial(main_kernel, sizes),
        out_shape=jax.ShapeDtypeStruct(sketch.shape, F32),
        in_specs=[pl.BlockSpec(memory_space=pltpu.HBM)] * 5,
        out_specs=anywhere,
        scratch_shapes=[
            pltpu.VMEM(diag_rows.shape, F32),
            pltpu.VMEM(couple_rows.shape, F32),
            pltpu.VMEM(noise_prec.shape, F32),
            pltpu.VMEM((steps, rows, sensors, cols), BF16),
            pltpu.VMEM((steps, points, sensors), BF16),
            pltpu.VMEM((steps, rows, cols, width), F32),
            pltpu.VMEM((steps, rows, cols, width), F32),
            pltpu.VMEM(edge_shape, BF16),
            pltpu.VMEM(edge_shape, BF16),
            pltpu.VMEM((2, 2, chunks + 1, points, width), BF16),
            pltpu.VMEM((chunks, sensors, 2 * width), F32),
            pltpu.VMEM((chunks, half, 2 * width), F32),
            pltpu.VMEM((chunks, half, 2 * width), BF16),
            pltpu.VMEM((chunks, (plane - 1) * piece, 2 * width), BF16),
            pltpu.VMEM((chunks, piece, 2 * width), BF16),
            pltpu.VMEM((chunks, nz - 1, piece, 2 * width), BF16),
            pltpu.VMEM((chunks, 2, piece, width), BF16),
            pltpu.VMEM((2, 2, chunks + 2, sensors, width), BF16),
            pltpu.VMEM((steps, points, width), F32),
            pltpu.VMEM(edge_shape, BF16),
            pltpu.VMEM(edge_shape, BF16),
            pltpu.VMEM((2, 2, rows, 1, cols), F32),
            pltpu.VMEM((rows + 4, cols, width), F32),
            pltpu.VMEM((rows + 2, cols, width), F32),
            *sweep_scratch,
            dma((2 * steps + 3,)),
            dma((2, 2)), dma((2, 2)),
            dma((steps, 2)), dma((steps, 2)),
            dma((chunks,)), dma((chunks,)),
            dma((chunks,)), dma((chunks,)),
            dma((chunks, nz)), dma((chunks, nz)),
            dma((chunks,)), dma((chunks,)),
            dma((chunks,)), dma((chunks,)),
            dma((steps, 2)), dma((steps, 2)),
            dma((steps,)),
        ],
        compiler_params=pltpu.CompilerParams(
            collective_id=0, has_side_effects=True, vmem_limit_bytes=48 * 1024 * 1024
        ),
        name="sketch_main",
    )(sketch, far(diag_rows), far(couple_rows), by_row, far(noise_prec))


def solution(mesh):
    placed = (
        P(None, "band", "tile", None, None),
        P("band", "tile", None),
        P("band", "tile", None),
        P(None, None, "band", "tile", None),
        P(),
    )
    return jax.shard_map(
        functools.partial(body, split(mesh)),
        mesh=mesh,
        in_specs=placed,
        out_specs=P(None, "band", "tile", None, None),
        check_vma=False,
    )
```

```python
import functools

import jax
import jax.numpy as jnp
from jax import lax
from jax.experimental import pallas as pl
from jax.experimental.pallas import tpu as pltpu
from jax.sharding import PartitionSpec as P

F32 = jnp.float32
BF16 = jnp.bfloat16
MESH = pl.DeviceIdType.MESH
COLS = 128
PAD = 8


def beside(ref, row):
    return ref[row, pl.ds(PAD - 1, COLS), :] + ref[row, pl.ds(PAD + 1, COLS), :]


def clear_pads(ref, rows):
    zero = jnp.zeros((PAD, ref.shape[2]), F32)
    for row in range(rows):
        ref[row, 0:PAD, :] = zero
        ref[row, PAD + COLS : 2 * PAD + COLS, :] = zero


def two_sweeps(rows, value, cpl, dia, coupled, again, swept, put):
    body = pl.ds(PAD, COLS)
    for j in range(rows + 4):
        coupled[j, body, :] = cpl[j] * value(j)
    for j in range(1, rows + 3):
        near = coupled[j - 1, body, :] + coupled[j + 1, body, :] + beside(coupled, j)
        once = dia[j - 1] * value(j) - cpl[j] * near
        swept[j - 1] = once
        again[j - 1, body, :] = cpl[j] * once
    for r in range(rows):
        q = r + 1
        near = again[q - 1, body, :] + again[q + 1, body, :] + beside(again, q)
        put(r, dia[q] * swept[q] - cpl[q + 1] * near)


class Place:
    def __init__(self, sizes):
        self.nyl, self.nyh, self.nx, self.nz = sizes
        self.tiles = self.nyh * self.nx * self.nz
        self.band = lax.axis_index("band")
        self.tile = lax.axis_index("tile")
        self.core = lax.rem(self.band, 2)
        self.z = lax.rem(self.tile, self.nz)
        self.plane = self.nyl * self.nyh * self.nx
        self.g = self.band // 2 * (self.nyh * self.nx) + self.tile // self.nz

    def twin(self):
        return (self.band + 1 - 2 * self.core, self.tile)

    def in_plane(self, d):
        sizes = (self.nyl, self.nyh, self.nx)
        inner = self.nyh * self.nx
        steps = (d // inner, d % inner // self.nx, d % self.nx)
        own = (self.g // inner, lax.rem(self.g, inner) // self.nx, lax.rem(self.g, self.nx))
        yl, yh, x = (lax.rem(o + step, n) for o, step, n in zip(own, steps, sizes))
        return yl * inner + yh * self.nx + x, (yl * 2 + self.core, (yh * self.nx + x) * self.nz + self.z)

    def plane_offsets(self):
        def hops(d):
            x = d % self.nx
            yl, yh = d // (self.nyh * self.nx), d // self.nx % self.nyh
            return min(x, self.nx - x) + (1 if yl else 2 * yh)

        return sorted(range(1, self.plane), key=hops, reverse=True)

    def z_offsets(self):
        return sorted(range(1, self.nz), key=lambda d: min(d, self.nz - d), reverse=True)

    def along_z(self, d):
        z = lax.rem(self.z + d, self.nz)
        return (self.band, self.tile - self.z + z)

    def row_neighbour(self, step):
        return (self.band, lax.rem(self.tile + step + self.tiles, self.tiles))


def remote(src, dst, send, recv, where):
    return pltpu.make_async_remote_copy(
        src_ref=src, dst_ref=dst, send_sem=send, recv_sem=recv, device_id=where, device_id_type=MESH
    )


def main_kernel(
    sizes,
    sketch_hbm, diag_hbm, couple_hbm, kern_hbm, prec_hbm,
    out_hbm,
    diag_ref, couple_ref, prec_ref,
    kv, kt, sk, field, stage, hin, smooth, total, pair_in, xsend, xin, zsend, zin, wsend, wgt, adj,
    edge_out, edge_in, coef_in, cpl, dia, coupled, again, swept,
    load_sem, coef_send, coef_recv, halo_send, halo_recv, pair_send, pair_recv, x_send, x_recv,
    z_send, z_recv, g_send, g_recv, p_send, p_recv, edge_send, edge_recv, out_sem,
):
    here = Place(sizes)
    steps, rows, sensors, _ = kv.shape
    points = rows * COLS
    chunks = steps // 2
    pairs = steps // 2
    half = sensors // 2
    piece = half // here.plane
    others = here.plane - 1
    zothers = here.nz - 1
    up, down = here.row_neighbour(-1), here.row_neighbour(1)
    has_up, has_down = here.tile > 0, here.tile < here.tiles - 1
    twin = here.twin()

    sketch_loads = [
        pltpu.make_async_copy(sketch_hbm.at[2 * p : 2 * p + 2, 0], sk.at[2 * p : 2 * p + 2], load_sem.at[p])
        for p in range(pairs)
    ]
    kern_loads = [
        pltpu.make_async_copy(kern_hbm.at[lag : lag + 4, 0], kv.at[lag : lag + 4], load_sem.at[pairs + i])
        for i, lag in enumerate(range(0, steps, 4))
    ]
    small_loads = [
        pltpu.make_async_copy(src, dst, load_sem.at[pairs + 2 + i])
        for i, (src, dst) in enumerate(
            ((couple_hbm, couple_ref), (diag_hbm, diag_ref), (prec_hbm, prec_ref))
        )
    ]
    barrier = pltpu.get_barrier_semaphore()
    greeted = [up, down, twin]
    greeted += [here.in_plane(d)[1] for d in range(1, here.plane)]
    greeted += [here.along_z(d) for d in range(1, here.nz)]
    for load in sketch_loads:
        load.start()
    for where in greeted:
        pl.semaphore_signal(barrier, inc=1, device_id=where, device_id_type=MESH)
    for load in small_loads + kern_loads:
        load.start()

    low = lax.broadcasted_iota(jnp.int32, (COLS, COLS), 1) < COLS // 2

    def turn(x):
        return pltpu.roll(x, COLS // 2, 1)

    def coef_copies(side, where):
        return [
            remote(ref, coef_in.at[side, i], coef_send.at[side], coef_recv.at[side], where)
            for i, ref in enumerate((couple_hbm, diag_hbm))
        ]

    def coef_bulk(side, where):
        return remote(coef_in.at[side], coef_in.at[side], coef_send.at[side], coef_recv.at[side], where)

    def halo_copy(f, side, where):
        return remote(
            stage.at[f, 1 - side], hin.at[f, side], halo_send.at[side], halo_recv.at[f, side], where
        )

    def edge_copy(f, side, where):
        return remote(
            edge_out.at[f, 1 - side], edge_in.at[f, side], edge_send.at[side], edge_recv.at[f, side], where
        )

    def send_halos(f, copy):
        @pl.when(has_up)
        def _():
            copy(f, 1, up).start()

        @pl.when(has_down)
        def _():
            copy(f, 0, down).start()

    def wait_halos(f, copy):
        @pl.when(has_up)
        def _():
            copy(f, 0, up).wait_recv()

        @pl.when(has_down)
        def _():
            copy(f, 1, down).wait_recv()

    def halos_sent(source, send):
        def one_side(side):
            block = source.at[:, 1 - side]
            remote(block, block, send.at[side], send.at[side], twin).wait_send()

        @pl.when(has_up)
        def _():
            one_side(1)

        @pl.when(has_down)
        def _():
            one_side(0)

    for p in range(pairs):
        sketch_loads[p].wait()

        for r in range(rows):
            first, second = sk[2 * p, r], sk[2 * p + 1, r]
            crossed = turn(jnp.where(low, second, first))
            field[p, r] = jnp.where(low, first, crossed)
            field[pairs + p, r] = jnp.where(low, crossed, second)
        for f in (p, pairs + p):
            stage[f, 0] = field[f, 0:2].reshape(2 * COLS, COLS).astype(BF16)
            stage[f, 1] = field[f, rows - 2 : rows].reshape(2 * COLS, COLS).astype(BF16)
        if p == 0:
            pl.semaphore_wait(barrier, len(greeted))

            @pl.when(has_up)
            def _():
                for copy in coef_copies(1, up):
                    copy.start()

            @pl.when(has_down)
            def _():
                for copy in coef_copies(0, down):
                    copy.start()

        send_halos(p, halo_copy)
    for p in range(pairs):
        send_halos(pairs + p, halo_copy)

    clear_pads(coupled, rows + 4)
    clear_pads(again, rows + 2)
    total[...] = jnp.zeros(total.shape, F32)
    adj[...] = jnp.zeros(adj.shape, F32)
    for h in range(2):
        smooth[h, 0, 0] = jnp.zeros((points, COLS), BF16)
        smooth[h, 1, 0] = jnp.zeros((points, COLS), BF16)
        wgt[h, 0, pairs] = jnp.zeros((sensors, COLS), BF16)
        wgt[h, 1, pairs + 1] = jnp.zeros((sensors, COLS), BF16)

    @pl.when(jnp.logical_not(has_up))
    def _():
        hin[:, 0] = jnp.zeros((steps, 2 * COLS, COLS), BF16)
        edge_in[:, 0] = jnp.zeros((steps, 2 * COLS, COLS), BF16)

    @pl.when(jnp.logical_not(has_down))
    def _():
        hin[:, 1] = jnp.zeros((steps, 2 * COLS, COLS), BF16)
        edge_in[:, 1] = jnp.zeros((steps, 2 * COLS, COLS), BF16)

    for load in small_loads:
        load.wait()

    def over_lanes(row):
        return jnp.broadcast_to(row, (COLS, COLS)).T

    for r in range(rows):
        cpl[r + 2] = over_lanes(couple_ref[r])
        dia[r + 1] = over_lanes(diag_ref[r])

    blank = jnp.zeros((COLS, COLS), F32)

    @pl.when(jnp.logical_not(has_up))
    def _():
        cpl[0] = blank
        cpl[1] = blank
        dia[0] = blank

    @pl.when(jnp.logical_not(has_down))
    def _():
        cpl[rows + 2] = blank
        cpl[rows + 3] = blank
        dia[rows + 1] = blank

    def flip(lag, carry):
        for r in range(rows):
            kt[lag, r * COLS : (r + 1) * COLS, :] = kv[lag, r].T
        return carry

    kern_loads[0].wait()
    lax.fori_loop(0, steps // 2, flip, 0)

    @pl.when(has_up)
    def _():
        coef_bulk(0, up).wait_recv()
        coef_bulk(1, up).wait_send()
        cpl[0] = over_lanes(coef_in[0, 0, rows - 2])
        cpl[1] = over_lanes(coef_in[0, 0, rows - 1])
        dia[0] = over_lanes(coef_in[0, 1, rows - 1])

    @pl.when(has_down)
    def _():
        coef_bulk(1, down).wait_recv()
        coef_bulk(0, down).wait_send()
        cpl[rows + 2] = over_lanes(coef_in[1, 0, 0])
        cpl[rows + 3] = over_lanes(coef_in[1, 0, 1])
        dia[rows + 1] = over_lanes(coef_in[1, 1, 0])

    my_half = pl.multiple_of(here.core * half, half)
    twin_half = pl.multiple_of(half - here.core * half, half)
    my_piece = pl.multiple_of(here.g * piece, piece)
    my_sensors = pl.multiple_of(here.core * half + here.g * piece, piece)

    def rows_of(own, edges, f):
        def value(j):
            if j < 2:
                return edges[f, 0, j * COLS : (j + 1) * COLS, :].astype(F32)
            if j < rows + 2:
                return own(j - 2)
            j = j - rows - 2
            return edges[f, 1, j * COLS : (j + 1) * COLS, :].astype(F32)

        return value

    def sweeps(value, put):
        two_sweeps(rows, value, cpl, dia, coupled, again, swept, put)

    def smooth_field(h, f):
        p = f - h * pairs
        wait_halos(f, halo_copy)

        def put(r, new):
            block = slice(r * COLS, (r + 1) * COLS)
            before = smooth[h, 0, p, block, :].astype(F32)
            smooth[h, 0, p + 1, block, :] = new.astype(BF16)
            smooth[h, 1, p + 1, block, :] = turn(jnp.where(low, new, before)).astype(BF16)

        sweeps(rows_of(lambda r: field[f, r], hin, f), put)

    def pair_copy(c):
        return remote(
            total.at[c, pl.ds(twin_half, half)], pair_in.at[c], pair_send, pair_recv.at[c], twin
        )

    def lags_dot(lags, lhs, rhs):
        left_side = jnp.concatenate([x for lag in lags for x in lhs(lag)], axis=1)
        right_side = jnp.concatenate([jnp.concatenate(rhs(lag), axis=1) for lag in lags], axis=0)
        return jnp.dot(left_side, right_side, preferred_element_type=F32)

    def at_step(step, wanted, *actions):
        @pl.when(step == wanted)
        def _():
            for action in actions:
                action()

    def forward(k, carry):
        h, i = k // 3, lax.rem(k, 3)
        q = (i + 1) // 2
        c = 2 * h + q
        fresh = i != 1
        start = jnp.where(fresh, 0, 4)

        at_step(k, 1, rest_of_kernel)
        at_step(k, 3, lambda: to_plane(0))

        @pl.when(fresh)
        def _():
            def per_field(f, inner):
                smooth_field(h, f)
                return inner

            lax.fori_loop(2 * c, 2 * c + 2, per_field, 0)

        at_step(k, 4, lambda: to_plane(1))
        at_step(k, 5, lambda: to_plane(2))
        first = 2 * q + 1 - start // 2

        def lhs(lag):
            return [kv[start + lag, r] for r in range(rows)]

        def rhs(lag):
            odd, at = lag % 2, first - lag // 2
            return [smooth[h, odd, at], smooth[h, odd, at + 1]]

        total[c] += lags_dot(range(4), lhs, rhs)

        @pl.when(fresh)
        def _():
            pair_copy(c).start()

        return carry

    def plane_copies(c):
        copies = []
        for d in here.plane_offsets():
            g, where = here.in_plane(d)
            copies.append(
                remote(
                    xsend.at[c, pl.ds(pl.multiple_of(g * piece, piece), piece)],
                    xin.at[c, pl.ds((d - 1) * piece, piece)],
                    x_send, x_recv.at[c], where,
                )
            )
        return copies

    def bulk(c, send, recv):
        block = xin.at[c]
        return remote(block, block, send, recv, twin)

    def to_plane(c):
        pair_copy(c).wait_recv()
        xsend[c] = (total[c, pl.ds(my_half, half)] + pair_in[c]).astype(BF16)
        for copy in plane_copies(c):
            copy.start()

    def z_copies(c):
        return [
            remote(zsend.at[c], zin.at[c, d - 1], z_send, z_recv.at[c], here.along_z(d))
            for d in here.z_offsets()
        ]

    def own_sum(c):
        rows_here = pl.ds(pl.multiple_of(my_half + my_piece, piece), piece)
        acc = total[c, rows_here] + pair_in[c, pl.ds(my_piece, piece)]
        for d in range(others):
            acc = acc + xin[c, d * piece : (d + 1) * piece].astype(F32)
        return acc

    def to_z(c):
        bulk(c, x_send, x_recv.at[c]).wait_recv()
        zsend[c] = own_sum(c).astype(BF16)
        for copy in z_copies(c):
            copy.start()

    def gather_copies(c):
        h, q = c // 2, c % 2
        return [
            remote(
                wsend.at[c],
                wgt.at[h, 0, pl.ds(2 * q, 2), pl.ds(my_sensors, piece)],
                g_send, g_recv.at[c], here.in_plane(d)[1],
            )
            for d in here.plane_offsets()
        ]

    spot = lax.broadcasted_iota(jnp.int32, (piece, sensors), 1)
    wanted = lax.broadcasted_iota(jnp.int32, (piece, sensors), 0) + my_sensors
    left = lax.broadcasted_iota(jnp.int32, (piece, COLS), 1) < COLS // 2

    def scale_of(t):
        return jnp.sum(jnp.where(spot == wanted, prec_ref[t : t + 1, :], 0.0), axis=1, keepdims=True)

    def to_gather(c):
        h, q = c // 2, c % 2
        remote(zin.at[c], zin.at[c], z_send, z_recv.at[c], twin).wait_recv()
        acc = own_sum(c)
        for d in range(zothers):
            acc = acc + zin[c, d].astype(F32)
        for i in range(2):
            t = 4 * q + 2 * i
            scale = jnp.where(left, scale_of(t), scale_of(t + 1))
            block = (acc[:, i * COLS : (i + 1) * COLS] * scale).astype(BF16)
            wsend[c, i] = block
            wgt[h, 0, 2 * q + i, pl.ds(my_sensors, piece), :] = block
        for copy in gather_copies(c):
            copy.start()

    def twin_copy(c):
        h, q = c // 2, c % 2
        block = wgt.at[h, 0, pl.ds(2 * q, 2), pl.ds(my_half, half)]
        return remote(block, block, p_send, p_recv.at[c], twin)

    def shift_blocks(c, base):
        h, q = c // 2, c % 2
        for p in (2, 3, 4) if q else (1,):
            for s in range(0, half, min(half, COLS)):
                block = pl.ds(pl.multiple_of(base + s, piece), min(half, COLS))
                mixed = jnp.where(
                    low[: min(half, COLS)],
                    wgt[h, 0, p, block, :].astype(F32),
                    wgt[h, 0, p - 1, block, :].astype(F32),
                )
                wgt[h, 1, p, block, :] = turn(mixed).astype(BF16)

    def to_twin(c):
        bulk(c, g_send, g_recv.at[c]).wait_recv()
        twin_copy(c).start()
        shift_blocks(c, my_half)

    def weights_in(c):
        twin_copy(c).wait_recv()
        shift_blocks(c, twin_half)

    def back(k, carry):
        h, i = k // 3, lax.rem(k, 3)
        q = jnp.where(i == 0, 1, 0)
        c = 2 * h + q
        start = jnp.where(i == 2, 4, 0)
        at_step(k, 2, lambda: to_twin(2))
        at_step(k, 3, lambda: to_twin(3), lambda: weights_in(2), lambda: weights_in(3))
        first = 2 * q + start // 2

        def lhs(lag):
            return [kt[start + lag]]

        def rhs(lag):
            odd, at = lag % 2, first + (lag + 1) // 2
            return [wgt[h, odd, at], wgt[h, odd, at + 1]]

        out = lags_dot(range(4), lhs, rhs)
        adj[2 * c] += out[:, :COLS]
        adj[2 * c + 1] += out[:, COLS:]

        @pl.when(i != 1)
        def _():
            for f in (2 * c, 2 * c + 1):
                edge_out[f, 0] = adj[f, 0 : 2 * COLS, :].astype(BF16)
                edge_out[f, 1] = adj[f, points - 2 * COLS : points, :].astype(BF16)
                send_halos(f, edge_copy)

        return carry

    def out_copy(t):
        return pltpu.make_async_copy(sk.at[t], out_hbm.at[t, 0], out_sem)

    def result(f):
        wait_halos(f, edge_copy)
        return rows_of(lambda r: adj[f, pl.ds(r * COLS, COLS), :], edge_in, f)

    def finish(k, carry):
        p = lax.rem(k + 2, pairs)
        f = k // pairs * pairs + p

        def put(r, new):
            field[f, r] = new

        sweeps(result(f), put)

        @pl.when(k >= pairs)
        def _():
            for r in range(rows):
                first, second = field[p, r], field[pairs + p, r]
                crossed = turn(jnp.where(low, second, first))
                sk[2 * p, r] = jnp.where(low, first, crossed)
                sk[2 * p + 1, r] = jnp.where(low, crossed, second)
            out_copy(2 * p).start()
            out_copy(2 * p + 1).start()

        return carry

    def rest_of_kernel():
        kern_loads[1].wait()

    lax.fori_loop(0, 6, forward, 0)
    to_z(0)
    to_plane(3)
    to_z(1)
    lax.fori_loop(steps // 2, steps, flip, 0)
    to_z(2)
    to_gather(0)
    to_gather(1)
    to_z(3)
    to_gather(2)
    to_twin(0)
    to_gather(3)
    to_twin(1)
    weights_in(0)
    weights_in(1)
    halos_sent(stage, halo_send)
    remote(pair_in, pair_in, pair_send, pair_send, twin).wait_send()
    remote(xin, xin, x_send, x_send, twin).wait_send()
    remote(zin, zin, z_send, z_send, twin).wait_send()
    lax.fori_loop(0, 6, back, 0)
    remote(xin, xin, g_send, g_send, twin).wait_send()
    remote(xsend, xsend, p_send, p_send, twin).wait_send()
    lax.fori_loop(0, steps, finish, 0)
    halos_sent(edge_out, edge_send)
    pltpu.make_async_copy(sk, out_hbm.at[:, 0], out_sem).wait()


def split(mesh):
    bands, tiles = mesh.shape["band"], mesh.shape["tile"]
    if tiles == 64:
        return (bands // 2, 2, 4, 8)
    return (bands // 2, 1, tiles // 2, 2)


def body(sizes, sketch, diag_coef, couple, kernel, noise_prec):
    steps, _, rows, cols, width = sketch.shape
    sensors = kernel.shape[1]
    points = rows * cols
    nyl, nyh, nx, nz = sizes
    plane = nyl * nyh * nx
    tiles = nyh * nx * nz
    half = sensors // 2
    piece = half // plane
    chunks = steps // 2
    by_row = jnp.transpose(kernel, (0, 2, 3, 1, 4))
    diag_rows = jnp.transpose(diag_coef, (1, 0, 2))
    couple_rows = jnp.transpose(couple, (1, 0, 2))
    anywhere = pl.BlockSpec(memory_space=pl.ANY)

    def far(x):
        return pltpu.with_memory_space_constraint(x, pltpu.HBM)

    dma = pltpu.SemaphoreType.DMA
    sweep_scratch = [
        pltpu.VMEM((rows + 4, cols + 2 * PAD, width), F32),
        pltpu.VMEM((rows + 2, cols + 2 * PAD, width), F32),
        pltpu.VMEM((rows + 2, cols, width), F32),
    ]
    edge_shape = (steps, 2, 2 * cols, width)
    return pl.pallas_call(
        functools.partial(main_kernel, sizes),
        out_shape=jax.ShapeDtypeStruct(sketch.shape, F32),
        in_specs=[pl.BlockSpec(memory_space=pltpu.HBM)] * 5,
        out_specs=anywhere,
        scratch_shapes=[
            pltpu.VMEM(diag_rows.shape, F32),
            pltpu.VMEM(couple_rows.shape, F32),
            pltpu.VMEM(noise_prec.shape, F32),
            pltpu.VMEM((steps, rows, sensors, cols), BF16),
            pltpu.VMEM((steps, points, sensors), BF16),
            pltpu.VMEM((steps, rows, cols, width), F32),
            pltpu.VMEM((steps, rows, cols, width), F32),
            pltpu.VMEM(edge_shape, BF16),
            pltpu.VMEM(edge_shape, BF16),
            pltpu.VMEM((2, 2, chunks + 1, points, width), BF16),
            pltpu.VMEM((chunks, sensors, 2 * width), F32),
            pltpu.VMEM((chunks, half, 2 * width), F32),
            pltpu.VMEM((chunks, half, 2 * width), BF16),
            pltpu.VMEM((chunks, (plane - 1) * piece, 2 * width), BF16),
            pltpu.VMEM((chunks, piece, 2 * width), BF16),
            pltpu.VMEM((chunks, nz - 1, piece, 2 * width), BF16),
            pltpu.VMEM((chunks, 2, piece, width), BF16),
            pltpu.VMEM((2, 2, chunks + 2, sensors, width), BF16),
            pltpu.VMEM((steps, points, width), F32),
            pltpu.VMEM(edge_shape, BF16),
            pltpu.VMEM(edge_shape, BF16),
            pltpu.VMEM((2, 2, rows, 1, cols), F32),
            pltpu.VMEM((rows + 4, cols, width), F32),
            pltpu.VMEM((rows + 2, cols, width), F32),
            *sweep_scratch,
            dma((chunks + 5,)),
            dma((2,)), dma((2,)),
            dma((2,)), dma((steps, 2)),
            dma(()), dma((chunks,)),
            dma(()), dma((chunks,)),
            dma(()), dma((chunks,)),
            dma(()), dma((chunks,)),
            dma(()), dma((chunks,)),
            dma((2,)), dma((steps, 2)),
            dma(()),
        ],
        compiler_params=pltpu.CompilerParams(
            collective_id=0, has_side_effects=True, vmem_limit_bytes=48 * 1024 * 1024
        ),
        name="sketch_main",
    )(sketch, far(diag_rows), far(couple_rows), by_row, far(noise_prec))


def solution(mesh):
    placed = (
        P(None, "band", "tile", None, None),
        P("band", "tile", None),
        P("band", "tile", None),
        P(None, None, "band", "tile", None),
        P(),
    )
    return jax.shard_map(
        functools.partial(body, split(mesh)),
        mesh=mesh,
        in_specs=placed,
        out_specs=P(None, "band", "tile", None, None),
        check_vma=False,
    )
```

```python
import functools

import jax
import jax.numpy as jnp
from jax import lax
from jax.experimental import pallas as pl
from jax.experimental.pallas import tpu as pltpu
from jax.sharding import PartitionSpec as P

F32 = jnp.float32
BF16 = jnp.bfloat16
MESH = pl.DeviceIdType.MESH
COLS = 128
PAD = 8


def beside(ref, row):
    return ref[row, pl.ds(PAD - 1, COLS), :] + ref[row, pl.ds(PAD + 1, COLS), :]


def clear_pads(ref, rows):
    zero = jnp.zeros((PAD, ref.shape[2]), F32)
    for row in range(rows):
        ref[row, 0:PAD, :] = zero
        ref[row, PAD + COLS : 2 * PAD + COLS, :] = zero


def two_sweeps(rows, value, cpl, dia, coupled, again, swept, put):
    body = pl.ds(PAD, COLS)
    for j in range(rows + 4):
        coupled[j, body, :] = cpl[j] * value(j)
    for j in range(1, rows + 3):
        near = coupled[j - 1, body, :] + coupled[j + 1, body, :] + beside(coupled, j)
        once = dia[j - 1] * value(j) - cpl[j] * near
        swept[j - 1] = once
        again[j - 1, body, :] = cpl[j] * once
    for r in range(rows):
        q = r + 1
        near = again[q - 1, body, :] + again[q + 1, body, :] + beside(again, q)
        put(r, dia[q] * swept[q] - cpl[q + 1] * near)


class Place:
    def __init__(self, sizes):
        self.nyl, self.nyh, self.nx, self.nz = sizes
        self.tiles = self.nyh * self.nx * self.nz
        self.band = lax.axis_index("band")
        self.tile = lax.axis_index("tile")
        self.core = lax.rem(self.band, 2)
        self.z = lax.rem(self.tile, self.nz)
        self.plane = self.nyl * self.nyh * self.nx
        self.g = self.band // 2 * (self.nyh * self.nx) + self.tile // self.nz

    def twin(self):
        return (self.band + 1 - 2 * self.core, self.tile)

    def in_plane(self, d):
        sizes = (self.nyl, self.nyh, self.nx)
        inner = self.nyh * self.nx
        steps = (d // inner, d % inner // self.nx, d % self.nx)
        own = (self.g // inner, lax.rem(self.g, inner) // self.nx, lax.rem(self.g, self.nx))
        yl, yh, x = (lax.rem(o + step, n) for o, step, n in zip(own, steps, sizes))
        return yl * inner + yh * self.nx + x, (yl * 2 + self.core, (yh * self.nx + x) * self.nz + self.z)

    def plane_offsets(self):
        def hops(d):
            x = d % self.nx
            yl, yh = d // (self.nyh * self.nx), d // self.nx % self.nyh
            return min(x, self.nx - x) + (1 if yl else 2 * yh)

        return sorted(range(1, self.plane), key=hops, reverse=True)

    def z_offsets(self):
        return sorted(range(1, self.nz), key=lambda d: min(d, self.nz - d), reverse=True)

    def along_z(self, d):
        z = lax.rem(self.z + d, self.nz)
        return (self.band, self.tile - self.z + z)

    def row_neighbour(self, step):
        return (self.band, lax.rem(self.tile + step + self.tiles, self.tiles))


def remote(src, dst, send, recv, where):
    return pltpu.make_async_remote_copy(
        src_ref=src, dst_ref=dst, send_sem=send, recv_sem=recv, device_id=where, device_id_type=MESH
    )


def main_kernel(
    sizes,
    sketch_hbm, diag_hbm, couple_hbm, kern_hbm, prec_hbm,
    out_hbm,
    diag_ref, couple_ref, prec_ref,
    kv, kt, sk, field, stage, hin, smooth, total, pair_in, xsend, xin, zsend, zin, wsend, wgt, adj,
    edge_out, edge_in, coef_in, cpl, dia, coupled, again, swept,
    load_sem, coef_send, coef_recv, halo_send, halo_recv, pair_send, pair_recv, x_send, x_recv,
    z_send, z_recv, g_send, g_recv, p_send, p_recv, edge_send, edge_recv, out_sem,
):
    here = Place(sizes)
    steps, rows, sensors, _ = kv.shape
    points = rows * COLS
    chunks = steps // 2
    pairs = steps // 2
    half = sensors // 2
    piece = half // here.plane
    others = here.plane - 1
    zothers = here.nz - 1
    up, down = here.row_neighbour(-1), here.row_neighbour(1)
    has_up, has_down = here.tile > 0, here.tile < here.tiles - 1
    twin = here.twin()

    sketch_loads = [
        pltpu.make_async_copy(sketch_hbm.at[2 * p : 2 * p + 2, 0], sk.at[2 * p : 2 * p + 2], load_sem.at[p])
        for p in range(pairs)
    ]
    kern_loads = [
        pltpu.make_async_copy(kern_hbm.at[lag : lag + 4, 0], kv.at[lag : lag + 4], load_sem.at[pairs + i])
        for i, lag in enumerate(range(0, steps, 4))
    ]
    small_loads = [
        pltpu.make_async_copy(src, dst, load_sem.at[pairs + 2 + i])
        for i, (src, dst) in enumerate(
            ((couple_hbm, couple_ref), (diag_hbm, diag_ref), (prec_hbm, prec_ref))
        )
    ]
    barrier = pltpu.get_barrier_semaphore()
    greeted = [up, down, twin]
    greeted += [here.in_plane(d)[1] for d in range(1, here.plane)]
    greeted += [here.along_z(d) for d in range(1, here.nz)]
    for load in sketch_loads:
        load.start()
    for where in greeted:
        pl.semaphore_signal(barrier, inc=1, device_id=where, device_id_type=MESH)
    for load in small_loads + kern_loads:
        load.start()

    low = lax.broadcasted_iota(jnp.int32, (COLS, COLS), 1) < COLS // 2

    def turn(x):
        return pltpu.roll(x, COLS // 2, 1)

    def coef_copies(side, where):
        return [
            remote(ref, coef_in.at[side, i], coef_send.at[side], coef_recv.at[side], where)
            for i, ref in enumerate((couple_hbm, diag_hbm))
        ]

    def coef_bulk(side, where):
        return remote(coef_in.at[side], coef_in.at[side], coef_send.at[side], coef_recv.at[side], where)

    def halo_copy(f, side, where):
        return remote(
            stage.at[f, 1 - side], hin.at[f, side], halo_send.at[side], halo_recv.at[f, side], where
        )

    def edge_copy(f, side, where):
        return remote(
            edge_out.at[f, 1 - side], edge_in.at[f, side], edge_send.at[side], edge_recv.at[f, side], where
        )

    def send_halos(f, copy):
        @pl.when(has_up)
        def _():
            copy(f, 1, up).start()

        @pl.when(has_down)
        def _():
            copy(f, 0, down).start()

    def wait_halos(f, copy):
        @pl.when(has_up)
        def _():
            copy(f, 0, up).wait_recv()

        @pl.when(has_down)
        def _():
            copy(f, 1, down).wait_recv()

    def halos_sent(source, send):
        def one_side(side):
            block = source.at[:, 1 - side]
            remote(block, block, send.at[side], send.at[side], twin).wait_send()

        @pl.when(has_up)
        def _():
            one_side(1)

        @pl.when(has_down)
        def _():
            one_side(0)

    for p in range(pairs):
        sketch_loads[p].wait()

        for r in range(rows):
            first, second = sk[2 * p, r], sk[2 * p + 1, r]
            crossed = turn(jnp.where(low, second, first))
            field[p, r] = jnp.where(low, first, crossed)
            field[pairs + p, r] = jnp.where(low, crossed, second)
        for f in (p, pairs + p):
            stage[f, 0] = field[f, 0:2].reshape(2 * COLS, COLS).astype(BF16)
            stage[f, 1] = field[f, rows - 2 : rows].reshape(2 * COLS, COLS).astype(BF16)
        if p == 0:
            pl.semaphore_wait(barrier, len(greeted))

            @pl.when(has_up)
            def _():
                for copy in coef_copies(1, up):
                    copy.start()

            @pl.when(has_down)
            def _():
                for copy in coef_copies(0, down):
                    copy.start()

        send_halos(p, halo_copy)
    for p in range(pairs):
        send_halos(pairs + p, halo_copy)

    clear_pads(coupled, rows + 4)
    clear_pads(again, rows + 2)
    total[...] = jnp.zeros(total.shape, F32)
    adj[...] = jnp.zeros(adj.shape, F32)
    for h in range(2):
        smooth[h, 0, 0] = jnp.zeros((points, COLS), BF16)
        smooth[h, 1, 0] = jnp.zeros((points, COLS), BF16)
        wgt[h, 0, pairs] = jnp.zeros((sensors, COLS), BF16)
        wgt[h, 1, pairs + 1] = jnp.zeros((sensors, COLS), BF16)

    @pl.when(jnp.logical_not(has_up))
    def _():
        hin[:, 0] = jnp.zeros((steps, 2 * COLS, COLS), BF16)
        edge_in[:, 0] = jnp.zeros((steps, 2 * COLS, COLS), BF16)

    @pl.when(jnp.logical_not(has_down))
    def _():
        hin[:, 1] = jnp.zeros((steps, 2 * COLS, COLS), BF16)
        edge_in[:, 1] = jnp.zeros((steps, 2 * COLS, COLS), BF16)

    for load in small_loads:
        load.wait()

    def over_lanes(row):
        return jnp.broadcast_to(row, (COLS, COLS)).T

    for r in range(rows):
        cpl[r + 2] = over_lanes(couple_ref[r])
        dia[r + 1] = over_lanes(diag_ref[r])

    blank = jnp.zeros((COLS, COLS), F32)

    @pl.when(jnp.logical_not(has_up))
    def _():
        cpl[0] = blank
        cpl[1] = blank
        dia[0] = blank

    @pl.when(jnp.logical_not(has_down))
    def _():
        cpl[rows + 2] = blank
        cpl[rows + 3] = blank
        dia[rows + 1] = blank

    def flip(lag, carry):
        for r in range(rows):
            kt[lag, r * COLS : (r + 1) * COLS, :] = kv[lag, r].T
        return carry

    kern_loads[0].wait()

    @pl.when(has_up)
    def _():
        coef_bulk(0, up).wait_recv()
        coef_bulk(1, up).wait_send()
        cpl[0] = over_lanes(coef_in[0, 0, rows - 2])
        cpl[1] = over_lanes(coef_in[0, 0, rows - 1])
        dia[0] = over_lanes(coef_in[0, 1, rows - 1])

    @pl.when(has_down)
    def _():
        coef_bulk(1, down).wait_recv()
        coef_bulk(0, down).wait_send()
        cpl[rows + 2] = over_lanes(coef_in[1, 0, 0])
        cpl[rows + 3] = over_lanes(coef_in[1, 0, 1])
        dia[rows + 1] = over_lanes(coef_in[1, 1, 0])

    my_half = pl.multiple_of(here.core * half, half)
    twin_half = pl.multiple_of(half - here.core * half, half)
    my_piece = pl.multiple_of(here.g * piece, piece)
    my_sensors = pl.multiple_of(here.core * half + here.g * piece, piece)

    def rows_of(own, edges, f):
        def value(j):
            if j < 2:
                return edges[f, 0, j * COLS : (j + 1) * COLS, :].astype(F32)
            if j < rows + 2:
                return own(j - 2)
            j = j - rows - 2
            return edges[f, 1, j * COLS : (j + 1) * COLS, :].astype(F32)

        return value

    def sweeps(value, put):
        two_sweeps(rows, value, cpl, dia, coupled, again, swept, put)

    def smooth_field(h, f):
        p = f - h * pairs
        wait_halos(f, halo_copy)

        def put(r, new):
            block = slice(r * COLS, (r + 1) * COLS)
            before = smooth[h, 0, p, block, :].astype(F32)
            smooth[h, 0, p + 1, block, :] = new.astype(BF16)
            smooth[h, 1, p + 1, block, :] = turn(jnp.where(low, new, before)).astype(BF16)

        sweeps(rows_of(lambda r: field[f, r], hin, f), put)

    def pair_copy(c):
        return remote(
            total.at[c, pl.ds(twin_half, half)], pair_in.at[c], pair_send, pair_recv.at[c], twin
        )

    def lags_dot(lags, lhs, rhs):
        left_side = jnp.concatenate([x for lag in lags for x in lhs(lag)], axis=1)
        right_side = jnp.concatenate([jnp.concatenate(rhs(lag), axis=1) for lag in lags], axis=0)
        return jnp.dot(left_side, right_side, preferred_element_type=F32)

    def at_step(step, wanted, *actions):
        @pl.when(step == wanted)
        def _():
            for action in actions:
                action()

    def forward(k, carry):
        h, i = k // 3, lax.rem(k, 3)
        q = (i + 1) // 2
        c = 2 * h + q
        fresh = i != 1
        start = jnp.where(fresh, 0, 4)

        at_step(k, 1, rest_of_kernel)
        at_step(k, 3, lambda: to_plane(0))

        @pl.when(fresh)
        def _():
            def per_field(f, inner):
                smooth_field(h, f)
                return inner

            lax.fori_loop(2 * c, 2 * c + 2, per_field, 0)

        at_step(k, 4, lambda: to_plane(1))
        at_step(k, 5, lambda: to_plane(2))
        first = 2 * q + 1 - start // 2

        def lhs(lag):
            return [kv[start + lag, r] for r in range(rows)]

        def rhs(lag):
            odd, at = lag % 2, first - lag // 2
            return [smooth[h, odd, at], smooth[h, odd, at + 1]]

        total[c] += lags_dot(range(4), lhs, rhs)

        @pl.when(fresh)
        def _():
            pair_copy(c).start()

        return carry

    def plane_copies(c):
        copies = []
        for d in here.plane_offsets():
            g, where = here.in_plane(d)
            copies.append(
                remote(
                    xsend.at[c, pl.ds(pl.multiple_of(g * piece, piece), piece)],
                    xin.at[c, pl.ds((d - 1) * piece, piece)],
                    x_send, x_recv.at[c], where,
                )
            )
        return copies

    def bulk(c, send, recv):
        block = xin.at[c]
        return remote(block, block, send, recv, twin)

    def to_plane(c):
        pair_copy(c).wait_recv()
        xsend[c] = (total[c, pl.ds(my_half, half)] + pair_in[c]).astype(BF16)
        for copy in plane_copies(c):
            copy.start()

    def z_copies(c):
        return [
            remote(zsend.at[c], zin.at[c, d - 1], z_send, z_recv.at[c], here.along_z(d))
            for d in here.z_offsets()
        ]

    def own_sum(c):
        rows_here = pl.ds(pl.multiple_of(my_half + my_piece, piece), piece)
        acc = total[c, rows_here] + pair_in[c, pl.ds(my_piece, piece)]
        for d in range(others):
            acc = acc + xin[c, d * piece : (d + 1) * piece].astype(F32)
        return acc

    def to_z(c):
        bulk(c, x_send, x_recv.at[c]).wait_recv()
        zsend[c] = own_sum(c).astype(BF16)
        for copy in z_copies(c):
            copy.start()

    def gather_copies(c):
        h, q = c // 2, c % 2
        return [
            remote(
                wsend.at[c],
                wgt.at[h, 0, pl.ds(2 * q, 2), pl.ds(my_sensors, piece)],
                g_send, g_recv.at[c], here.in_plane(d)[1],
            )
            for d in here.plane_offsets()
        ]

    spot = lax.broadcasted_iota(jnp.int32, (piece, sensors), 1)
    wanted = lax.broadcasted_iota(jnp.int32, (piece, sensors), 0) + my_sensors
    left = lax.broadcasted_iota(jnp.int32, (piece, COLS), 1) < COLS // 2

    def scale_of(t):
        return jnp.sum(jnp.where(spot == wanted, prec_ref[t : t + 1, :], 0.0), axis=1, keepdims=True)

    def to_gather(c):
        h, q = c // 2, c % 2
        remote(zin.at[c], zin.at[c], z_send, z_recv.at[c], twin).wait_recv()
        acc = own_sum(c)
        for d in range(zothers):
            acc = acc + zin[c, d].astype(F32)
        for i in range(2):
            t = 4 * q + 2 * i
            scale = jnp.where(left, scale_of(t), scale_of(t + 1))
            block = (acc[:, i * COLS : (i + 1) * COLS] * scale).astype(BF16)
            wsend[c, i] = block
            wgt[h, 0, 2 * q + i, pl.ds(my_sensors, piece), :] = block
        for copy in gather_copies(c):
            copy.start()

    def twin_copy(c):
        h, q = c // 2, c % 2
        block = wgt.at[h, 0, pl.ds(2 * q, 2), pl.ds(my_half, half)]
        return remote(block, block, p_send, p_recv.at[c], twin)

    def shift_blocks(c, base):
        h, q = c // 2, c % 2
        for p in (2, 3, 4) if q else (1,):
            for s in range(0, half, min(half, COLS)):
                block = pl.ds(pl.multiple_of(base + s, piece), min(half, COLS))
                mixed = jnp.where(
                    low[: min(half, COLS)],
                    wgt[h, 0, p, block, :].astype(F32),
                    wgt[h, 0, p - 1, block, :].astype(F32),
                )
                wgt[h, 1, p, block, :] = turn(mixed).astype(BF16)

    def to_twin(c):
        bulk(c, g_send, g_recv.at[c]).wait_recv()
        twin_copy(c).start()
        shift_blocks(c, my_half)

    def weights_in(c):
        twin_copy(c).wait_recv()
        shift_blocks(c, twin_half)

    def back(k, carry):
        h, i = k // 3, lax.rem(k, 3)
        q = jnp.where(i == 0, 1, 0)
        c = 2 * h + q
        start = jnp.where(i == 2, 4, 0)
        at_step(k, 2, lambda: to_twin(2), lambda: to_twin(3))
        at_step(k, 3, lambda: weights_in(2), lambda: weights_in(3))
        first = 2 * q + start // 2

        def lhs(lag):
            return [kt[start + lag]]

        def rhs(lag):
            odd, at = lag % 2, first + (lag + 1) // 2
            return [wgt[h, odd, at], wgt[h, odd, at + 1]]

        out = lags_dot(range(4), lhs, rhs)
        adj[2 * c] += out[:, :COLS]
        adj[2 * c + 1] += out[:, COLS:]

        @pl.when(i != 1)
        def _():
            for f in (2 * c, 2 * c + 1):
                edge_out[f, 0] = adj[f, 0 : 2 * COLS, :].astype(BF16)
                edge_out[f, 1] = adj[f, points - 2 * COLS : points, :].astype(BF16)
                send_halos(f, edge_copy)

        return carry

    def out_copy(t):
        return pltpu.make_async_copy(sk.at[t], out_hbm.at[t, 0], out_sem)

    def result(f):
        wait_halos(f, edge_copy)
        return rows_of(lambda r: adj[f, pl.ds(r * COLS, COLS), :], edge_in, f)

    def finish(k, carry):
        p = lax.rem(k + 2, pairs)
        f = k // pairs * pairs + p

        def put(r, new):
            field[f, r] = new

        sweeps(result(f), put)

        @pl.when(k >= pairs)
        def _():
            for r in range(rows):
                first, second = field[p, r], field[pairs + p, r]
                crossed = turn(jnp.where(low, second, first))
                sk[2 * p, r] = jnp.where(low, first, crossed)
                sk[2 * p + 1, r] = jnp.where(low, crossed, second)
            out_copy(2 * p).start()
            out_copy(2 * p + 1).start()

        return carry

    def rest_of_kernel():
        kern_loads[1].wait()

    lax.fori_loop(0, 6, forward, 0)
    to_z(0)
    to_plane(3)
    lax.fori_loop(0, steps // 2, flip, 0)
    to_z(1)
    lax.fori_loop(steps // 2, steps, flip, 0)
    to_z(2)
    to_gather(0)
    to_z(3)
    to_gather(1)
    to_gather(2)
    to_twin(0)
    to_gather(3)
    to_twin(1)
    weights_in(0)
    weights_in(1)
    halos_sent(stage, halo_send)
    remote(pair_in, pair_in, pair_send, pair_send, twin).wait_send()
    remote(xin, xin, x_send, x_send, twin).wait_send()
    remote(zin, zin, z_send, z_send, twin).wait_send()
    lax.fori_loop(0, 6, back, 0)
    remote(xin, xin, g_send, g_send, twin).wait_send()
    remote(xsend, xsend, p_send, p_send, twin).wait_send()
    lax.fori_loop(0, steps, finish, 0)
    halos_sent(edge_out, edge_send)
    pltpu.make_async_copy(sk, out_hbm.at[:, 0], out_sem).wait()


def split(mesh):
    bands, tiles = mesh.shape["band"], mesh.shape["tile"]
    if tiles == 64:
        return (bands // 2, 2, 4, 8)
    return (bands // 2, 1, tiles // 2, 2)


def body(sizes, sketch, diag_coef, couple, kernel, noise_prec):
    steps, _, rows, cols, width = sketch.shape
    sensors = kernel.shape[1]
    points = rows * cols
    nyl, nyh, nx, nz = sizes
    plane = nyl * nyh * nx
    tiles = nyh * nx * nz
    half = sensors // 2
    piece = half // plane
    chunks = steps // 2
    by_row = jnp.transpose(kernel, (0, 2, 3, 1, 4))
    diag_rows = jnp.transpose(diag_coef, (1, 0, 2))
    couple_rows = jnp.transpose(couple, (1, 0, 2))
    anywhere = pl.BlockSpec(memory_space=pl.ANY)

    def far(x):
        return pltpu.with_memory_space_constraint(x, pltpu.HBM)

    dma = pltpu.SemaphoreType.DMA
    sweep_scratch = [
        pltpu.VMEM((rows + 4, cols + 2 * PAD, width), F32),
        pltpu.VMEM((rows + 2, cols + 2 * PAD, width), F32),
        pltpu.VMEM((rows + 2, cols, width), F32),
    ]
    edge_shape = (steps, 2, 2 * cols, width)
    return pl.pallas_call(
        functools.partial(main_kernel, sizes),
        out_shape=jax.ShapeDtypeStruct(sketch.shape, F32),
        in_specs=[pl.BlockSpec(memory_space=pltpu.HBM)] * 5,
        out_specs=anywhere,
        scratch_shapes=[
            pltpu.VMEM(diag_rows.shape, F32),
            pltpu.VMEM(couple_rows.shape, F32),
            pltpu.VMEM(noise_prec.shape, F32),
            pltpu.VMEM((steps, rows, sensors, cols), BF16),
            pltpu.VMEM((steps, points, sensors), BF16),
            pltpu.VMEM((steps, rows, cols, width), F32),
            pltpu.VMEM((steps, rows, cols, width), F32),
            pltpu.VMEM(edge_shape, BF16),
            pltpu.VMEM(edge_shape, BF16),
            pltpu.VMEM((2, 2, chunks + 1, points, width), BF16),
            pltpu.VMEM((chunks, sensors, 2 * width), F32),
            pltpu.VMEM((chunks, half, 2 * width), F32),
            pltpu.VMEM((chunks, half, 2 * width), BF16),
            pltpu.VMEM((chunks, (plane - 1) * piece, 2 * width), BF16),
            pltpu.VMEM((chunks, piece, 2 * width), BF16),
            pltpu.VMEM((chunks, nz - 1, piece, 2 * width), BF16),
            pltpu.VMEM((chunks, 2, piece, width), BF16),
            pltpu.VMEM((2, 2, chunks + 2, sensors, width), BF16),
            pltpu.VMEM((steps, points, width), F32),
            pltpu.VMEM(edge_shape, BF16),
            pltpu.VMEM(edge_shape, BF16),
            pltpu.VMEM((2, 2, rows, 1, cols), F32),
            pltpu.VMEM((rows + 4, cols, width), F32),
            pltpu.VMEM((rows + 2, cols, width), F32),
            *sweep_scratch,
            dma((chunks + 5,)),
            dma((2,)), dma((2,)),
            dma((2,)), dma((steps, 2)),
            dma(()), dma((chunks,)),
            dma(()), dma((chunks,)),
            dma(()), dma((chunks,)),
            dma(()), dma((chunks,)),
            dma(()), dma((chunks,)),
            dma((2,)), dma((steps, 2)),
            dma(()),
        ],
        compiler_params=pltpu.CompilerParams(
            collective_id=0, has_side_effects=True, vmem_limit_bytes=48 * 1024 * 1024
        ),
        name="sketch_main",
    )(sketch, far(diag_rows), far(couple_rows), by_row, far(noise_prec))


def solution(mesh):
    placed = (
        P(None, "band", "tile", None, None),
        P("band", "tile", None),
        P("band", "tile", None),
        P(None, None, "band", "tile", None),
        P(),
    )
    return jax.shard_map(
        functools.partial(body, split(mesh)),
        mesh=mesh,
        in_specs=placed,
        out_specs=P(None, "band", "tile", None, None),
        check_vma=False,
    )
```

```python
import functools

import jax
import jax.numpy as jnp
from jax import lax
from jax.experimental import pallas as pl
from jax.experimental.pallas import tpu as pltpu
from jax.sharding import PartitionSpec as P

F32 = jnp.float32
BF16 = jnp.bfloat16
MESH = pl.DeviceIdType.MESH
COLS = 128
PAD = 8


def beside(ref, row):
    return ref[row, pl.ds(PAD - 1, COLS), :] + ref[row, pl.ds(PAD + 1, COLS), :]


def clear_pads(ref, rows):
    zero = jnp.zeros((PAD, ref.shape[2]), F32)
    for row in range(rows):
        ref[row, 0:PAD, :] = zero
        ref[row, PAD + COLS : 2 * PAD + COLS, :] = zero


def two_sweeps(rows, value, cpl, dia, coupled, again, swept, put):
    body = pl.ds(PAD, COLS)
    for j in range(rows + 4):
        coupled[j, body, :] = cpl[j] * value(j)
    for j in range(1, rows + 3):
        near = coupled[j - 1, body, :] + coupled[j + 1, body, :] + beside(coupled, j)
        once = dia[j - 1] * value(j) - cpl[j] * near
        swept[j - 1] = once
        again[j - 1, body, :] = cpl[j] * once
    for r in range(rows):
        q = r + 1
        near = again[q - 1, body, :] + again[q + 1, body, :] + beside(again, q)
        put(r, dia[q] * swept[q] - cpl[q + 1] * near)


class Place:
    def __init__(self, sizes):
        self.nyl, self.nyh, self.nx, self.nz = sizes
        self.tiles = self.nyh * self.nx * self.nz
        self.band = lax.axis_index("band")
        self.tile = lax.axis_index("tile")
        self.core = lax.rem(self.band, 2)
        self.z = lax.rem(self.tile, self.nz)
        self.plane = self.nyl * self.nyh * self.nx
        self.g = self.band // 2 * (self.nyh * self.nx) + self.tile // self.nz

    def twin(self):
        return (self.band + 1 - 2 * self.core, self.tile)

    def in_plane(self, d):
        sizes = (self.nyl, self.nyh, self.nx)
        inner = self.nyh * self.nx
        steps = (d // inner, d % inner // self.nx, d % self.nx)
        own = (self.g // inner, lax.rem(self.g, inner) // self.nx, lax.rem(self.g, self.nx))
        yl, yh, x = (lax.rem(o + step, n) for o, step, n in zip(own, steps, sizes))
        return yl * inner + yh * self.nx + x, (yl * 2 + self.core, (yh * self.nx + x) * self.nz + self.z)

    def plane_offsets(self):
        def hops(d):
            x = d % self.nx
            yl, yh = d // (self.nyh * self.nx), d // self.nx % self.nyh
            return min(x, self.nx - x) + (1 if yl else 2 * yh)

        return sorted(range(1, self.plane), key=hops, reverse=True)

    def z_offsets(self):
        return sorted(range(1, self.nz), key=lambda d: min(d, self.nz - d), reverse=True)

    def along_z(self, d):
        z = lax.rem(self.z + d, self.nz)
        return (self.band, self.tile - self.z + z)

    def row_neighbour(self, step):
        return (self.band, lax.rem(self.tile + step + self.tiles, self.tiles))


def remote(src, dst, send, recv, where):
    return pltpu.make_async_remote_copy(
        src_ref=src, dst_ref=dst, send_sem=send, recv_sem=recv, device_id=where, device_id_type=MESH
    )


def main_kernel(
    sizes,
    sketch_hbm, diag_hbm, couple_hbm, kern_hbm, prec_hbm,
    out_hbm,
    diag_ref, couple_ref, prec_ref,
    kv, kt, sk, field, stage, hin, smooth, total, pair_in, xsend, xin, zsend, zin, wsend, wgt, adj,
    edge_out, edge_in, coef_in, cpl, dia, coupled, again, swept,
    load_sem, coef_send, coef_recv, halo_send, halo_recv, pair_send, pair_recv, x_send, x_recv,
    z_send, z_recv, g_send, g_recv, p_send, p_recv, edge_send, edge_recv, out_sem,
):
    here = Place(sizes)
    steps, rows, sensors, _ = kv.shape
    points = rows * COLS
    chunks = steps // 2
    pairs = steps // 2
    half = sensors // 2
    piece = half // here.plane
    others = here.plane - 1
    zothers = here.nz - 1
    up, down = here.row_neighbour(-1), here.row_neighbour(1)
    has_up, has_down = here.tile > 0, here.tile < here.tiles - 1
    twin = here.twin()

    sketch_loads = [
        pltpu.make_async_copy(sketch_hbm.at[2 * p : 2 * p + 2, 0], sk.at[2 * p : 2 * p + 2], load_sem.at[p])
        for p in range(pairs)
    ]
    kern_loads = [
        pltpu.make_async_copy(kern_hbm.at[lag : lag + 4, 0], kv.at[lag : lag + 4], load_sem.at[pairs + i])
        for i, lag in enumerate(range(0, steps, 4))
    ]
    small_loads = [
        pltpu.make_async_copy(src, dst, load_sem.at[pairs + 2 + i])
        for i, (src, dst) in enumerate(
            ((couple_hbm, couple_ref), (diag_hbm, diag_ref), (prec_hbm, prec_ref))
        )
    ]
    barrier = pltpu.get_barrier_semaphore()
    greeted = [up, down, twin]
    greeted += [here.in_plane(d)[1] for d in range(1, here.plane)]
    greeted += [here.along_z(d) for d in range(1, here.nz)]
    for load in sketch_loads:
        load.start()
    for where in greeted:
        pl.semaphore_signal(barrier, inc=1, device_id=where, device_id_type=MESH)
    for load in small_loads + kern_loads:
        load.start()

    low = lax.broadcasted_iota(jnp.int32, (COLS, COLS), 1) < COLS // 2

    def turn(x):
        return pltpu.roll(x, COLS // 2, 1)

    def coef_copies(side, where):
        return [
            remote(ref, coef_in.at[side, i], coef_send.at[side], coef_recv.at[side], where)
            for i, ref in enumerate((couple_hbm, diag_hbm))
        ]

    def coef_bulk(side, where):
        return remote(coef_in.at[side], coef_in.at[side], coef_send.at[side], coef_recv.at[side], where)

    def halo_copy(f, side, where):
        return remote(
            stage.at[f, 1 - side], hin.at[f, side], halo_send.at[side], halo_recv.at[f, side], where
        )

    def edge_copy(f, side, where):
        return remote(
            edge_out.at[f, 1 - side], edge_in.at[f, side], edge_send.at[side], edge_recv.at[f, side], where
        )

    def send_halos(f, copy):
        @pl.when(has_up)
        def _():
            copy(f, 1, up).start()

        @pl.when(has_down)
        def _():
            copy(f, 0, down).start()

    def wait_halos(f, copy):
        @pl.when(has_up)
        def _():
            copy(f, 0, up).wait_recv()

        @pl.when(has_down)
        def _():
            copy(f, 1, down).wait_recv()

    def halos_sent(source, send):
        def one_side(side):
            block = source.at[:, 1 - side]
            remote(block, block, send.at[side], send.at[side], twin).wait_send()

        @pl.when(has_up)
        def _():
            one_side(1)

        @pl.when(has_down)
        def _():
            one_side(0)

    for p in range(pairs):
        sketch_loads[p].wait()

        for r in range(rows):
            first, second = sk[2 * p, r], sk[2 * p + 1, r]
            crossed = turn(jnp.where(low, second, first))
            field[p, r] = jnp.where(low, first, crossed)
            field[pairs + p, r] = jnp.where(low, crossed, second)
        for f in (p, pairs + p):
            stage[f, 0] = field[f, 0:2].reshape(2 * COLS, COLS).astype(BF16)
            stage[f, 1] = field[f, rows - 2 : rows].reshape(2 * COLS, COLS).astype(BF16)
        if p == 0:
            pl.semaphore_wait(barrier, len(greeted))

            @pl.when(has_up)
            def _():
                for copy in coef_copies(1, up):
                    copy.start()

            @pl.when(has_down)
            def _():
                for copy in coef_copies(0, down):
                    copy.start()

        send_halos(p, halo_copy)
    for p in range(pairs):
        send_halos(pairs + p, halo_copy)

    clear_pads(coupled, rows + 4)
    clear_pads(again, rows + 2)
    total[...] = jnp.zeros(total.shape, F32)
    adj[...] = jnp.zeros(adj.shape, F32)
    for h in range(2):
        smooth[h, 0, 0] = jnp.zeros((points, COLS), BF16)
        smooth[h, 1, 0] = jnp.zeros((points, COLS), BF16)
        wgt[h, 0, pairs] = jnp.zeros((sensors, COLS), BF16)
        wgt[h, 1, pairs + 1] = jnp.zeros((sensors, COLS), BF16)

    @pl.when(jnp.logical_not(has_up))
    def _():
        hin[:, 0] = jnp.zeros((steps, 2 * COLS, COLS), BF16)
        edge_in[:, 0] = jnp.zeros((steps, 2 * COLS, COLS), BF16)

    @pl.when(jnp.logical_not(has_down))
    def _():
        hin[:, 1] = jnp.zeros((steps, 2 * COLS, COLS), BF16)
        edge_in[:, 1] = jnp.zeros((steps, 2 * COLS, COLS), BF16)

    for load in small_loads:
        load.wait()

    def over_lanes(row):
        return jnp.broadcast_to(row, (COLS, COLS)).T

    for r in range(rows):
        cpl[r + 2] = over_lanes(couple_ref[r])
        dia[r + 1] = over_lanes(diag_ref[r])

    blank = jnp.zeros((COLS, COLS), F32)

    @pl.when(jnp.logical_not(has_up))
    def _():
        cpl[0] = blank
        cpl[1] = blank
        dia[0] = blank

    @pl.when(jnp.logical_not(has_down))
    def _():
        cpl[rows + 2] = blank
        cpl[rows + 3] = blank
        dia[rows + 1] = blank

    def flip(lag, carry):
        for r in range(rows):
            kt[lag, r * COLS : (r + 1) * COLS, :] = kv[lag, r].T
        return carry

    kern_loads[0].wait()

    @pl.when(has_up)
    def _():
        coef_bulk(0, up).wait_recv()
        coef_bulk(1, up).wait_send()
        cpl[0] = over_lanes(coef_in[0, 0, rows - 2])
        cpl[1] = over_lanes(coef_in[0, 0, rows - 1])
        dia[0] = over_lanes(coef_in[0, 1, rows - 1])

    @pl.when(has_down)
    def _():
        coef_bulk(1, down).wait_recv()
        coef_bulk(0, down).wait_send()
        cpl[rows + 2] = over_lanes(coef_in[1, 0, 0])
        cpl[rows + 3] = over_lanes(coef_in[1, 0, 1])
        dia[rows + 1] = over_lanes(coef_in[1, 1, 0])

    my_half = pl.multiple_of(here.core * half, half)
    twin_half = pl.multiple_of(half - here.core * half, half)
    my_piece = pl.multiple_of(here.g * piece, piece)
    my_sensors = pl.multiple_of(here.core * half + here.g * piece, piece)

    def rows_of(own, edges, f):
        def value(j):
            if j < 2:
                return edges[f, 0, j * COLS : (j + 1) * COLS, :].astype(F32)
            if j < rows + 2:
                return own(j - 2)
            j = j - rows - 2
            return edges[f, 1, j * COLS : (j + 1) * COLS, :].astype(F32)

        return value

    def sweeps(value, put):
        two_sweeps(rows, value, cpl, dia, coupled, again, swept, put)

    def smooth_field(h, f):
        p = f - h * pairs
        wait_halos(f, halo_copy)

        def put(r, new):
            block = slice(r * COLS, (r + 1) * COLS)
            before = smooth[h, 0, p, block, :].astype(F32)
            smooth[h, 0, p + 1, block, :] = new.astype(BF16)
            smooth[h, 1, p + 1, block, :] = turn(jnp.where(low, new, before)).astype(BF16)

        sweeps(rows_of(lambda r: field[f, r], hin, f), put)

    def pair_copy(c):
        return remote(
            total.at[c, pl.ds(twin_half, half)], pair_in.at[c], pair_send, pair_recv.at[c], twin
        )

    def lags_dot(lags, lhs, rhs):
        left_side = jnp.concatenate([x for lag in lags for x in lhs(lag)], axis=1)
        right_side = jnp.concatenate([jnp.concatenate(rhs(lag), axis=1) for lag in lags], axis=0)
        return jnp.dot(left_side, right_side, preferred_element_type=F32)

    def at_step(step, wanted, *actions):
        @pl.when(step == wanted)
        def _():
            for action in actions:
                action()

    def forward(k, carry):
        h, i = k // 3, lax.rem(k, 3)
        q = (i + 1) // 2
        c = 2 * h + q
        fresh = i != 1
        start = jnp.where(fresh, 0, 4)

        at_step(k, 1, rest_of_kernel)
        at_step(k, 3, lambda: to_plane(0))

        @pl.when(fresh)
        def _():
            def per_field(f, inner):
                smooth_field(h, f)
                return inner

            lax.fori_loop(2 * c, 2 * c + 2, per_field, 0)

        at_step(k, 3, lambda: to_plane(1))
        at_step(k, 5, lambda: to_plane(2))
        first = 2 * q + 1 - start // 2

        def lhs(lag):
            return [kv[start + lag, r] for r in range(rows)]

        def rhs(lag):
            odd, at = lag % 2, first - lag // 2
            return [smooth[h, odd, at], smooth[h, odd, at + 1]]

        total[c] += lags_dot(range(4), lhs, rhs)

        @pl.when(fresh)
        def _():
            pair_copy(c).start()

        return carry

    def plane_copies(c):
        copies = []
        for d in here.plane_offsets():
            g, where = here.in_plane(d)
            copies.append(
                remote(
                    xsend.at[c, pl.ds(pl.multiple_of(g * piece, piece), piece)],
                    xin.at[c, pl.ds((d - 1) * piece, piece)],
                    x_send, x_recv.at[c], where,
                )
            )
        return copies

    def bulk(c, send, recv):
        block = xin.at[c]
        return remote(block, block, send, recv, twin)

    def to_plane(c):
        pair_copy(c).wait_recv()
        xsend[c] = (total[c, pl.ds(my_half, half)] + pair_in[c]).astype(BF16)
        for copy in plane_copies(c):
            copy.start()

    def z_copies(c):
        return [
            remote(zsend.at[c], zin.at[c, d - 1], z_send, z_recv.at[c], here.along_z(d))
            for d in here.z_offsets()
        ]

    def own_sum(c):
        rows_here = pl.ds(pl.multiple_of(my_half + my_piece, piece), piece)
        acc = total[c, rows_here] + pair_in[c, pl.ds(my_piece, piece)]
        for d in range(others):
            acc = acc + xin[c, d * piece : (d + 1) * piece].astype(F32)
        return acc

    def to_z(c):
        bulk(c, x_send, x_recv.at[c]).wait_recv()
        zsend[c] = own_sum(c).astype(BF16)
        for copy in z_copies(c):
            copy.start()

    def gather_copies(c):
        h, q = c // 2, c % 2
        return [
            remote(
                wsend.at[c],
                wgt.at[h, 0, pl.ds(2 * q, 2), pl.ds(my_sensors, piece)],
                g_send, g_recv.at[c], here.in_plane(d)[1],
            )
            for d in here.plane_offsets()
        ]

    spot = lax.broadcasted_iota(jnp.int32, (piece, sensors), 1)
    wanted = lax.broadcasted_iota(jnp.int32, (piece, sensors), 0) + my_sensors
    left = lax.broadcasted_iota(jnp.int32, (piece, COLS), 1) < COLS // 2

    def scale_of(t):
        return jnp.sum(jnp.where(spot == wanted, prec_ref[t : t + 1, :], 0.0), axis=1, keepdims=True)

    def to_gather(c):
        h, q = c // 2, c % 2
        remote(zin.at[c], zin.at[c], z_send, z_recv.at[c], twin).wait_recv()
        acc = own_sum(c)
        for d in range(zothers):
            acc = acc + zin[c, d].astype(F32)
        for i in range(2):
            t = 4 * q + 2 * i
            scale = jnp.where(left, scale_of(t), scale_of(t + 1))
            block = (acc[:, i * COLS : (i + 1) * COLS] * scale).astype(BF16)
            wsend[c, i] = block
            wgt[h, 0, 2 * q + i, pl.ds(my_sensors, piece), :] = block
        for copy in gather_copies(c):
            copy.start()

    def twin_copy(c):
        h, q = c // 2, c % 2
        block = wgt.at[h, 0, pl.ds(2 * q, 2), pl.ds(my_half, half)]
        return remote(block, block, p_send, p_recv.at[c], twin)

    def shift_blocks(c, base):
        h, q = c // 2, c % 2
        for p in (2, 3, 4) if q else (1,):
            for s in range(0, half, min(half, COLS)):
                block = pl.ds(pl.multiple_of(base + s, piece), min(half, COLS))
                mixed = jnp.where(
                    low[: min(half, COLS)],
                    wgt[h, 0, p, block, :].astype(F32),
                    wgt[h, 0, p - 1, block, :].astype(F32),
                )
                wgt[h, 1, p, block, :] = turn(mixed).astype(BF16)

    def to_twin(c):
        bulk(c, g_send, g_recv.at[c]).wait_recv()
        twin_copy(c).start()
        shift_blocks(c, my_half)

    def weights_in(c):
        twin_copy(c).wait_recv()
        shift_blocks(c, twin_half)

    def back(k, carry):
        h, i = k // 3, lax.rem(k, 3)
        q = jnp.where(i == 0, 1, 0)
        c = 2 * h + q
        start = jnp.where(i == 2, 4, 0)
        at_step(k, 2, lambda: to_twin(2))
        at_step(k, 3, lambda: to_twin(3), lambda: weights_in(2), lambda: weights_in(3))
        first = 2 * q + start // 2

        def lhs(lag):
            return [kt[start + lag]]

        def rhs(lag):
            odd, at = lag % 2, first + (lag + 1) // 2
            return [wgt[h, odd, at], wgt[h, odd, at + 1]]

        out = lags_dot(range(4), lhs, rhs)
        adj[2 * c] += out[:, :COLS]
        adj[2 * c + 1] += out[:, COLS:]

        @pl.when(i != 1)
        def _():
            for f in (2 * c, 2 * c + 1):
                edge_out[f, 0] = adj[f, 0 : 2 * COLS, :].astype(BF16)
                edge_out[f, 1] = adj[f, points - 2 * COLS : points, :].astype(BF16)
                send_halos(f, edge_copy)

        return carry

    def out_copy(t):
        return pltpu.make_async_copy(sk.at[t], out_hbm.at[t, 0], out_sem)

    def result(f):
        wait_halos(f, edge_copy)
        return rows_of(lambda r: adj[f, pl.ds(r * COLS, COLS), :], edge_in, f)

    def finish(k, carry):
        p = lax.rem(k + 2, pairs)
        f = k // pairs * pairs + p

        def put(r, new):
            field[f, r] = new

        sweeps(result(f), put)

        @pl.when(k >= pairs)
        def _():
            for r in range(rows):
                first, second = field[p, r], field[pairs + p, r]
                crossed = turn(jnp.where(low, second, first))
                sk[2 * p, r] = jnp.where(low, first, crossed)
                sk[2 * p + 1, r] = jnp.where(low, crossed, second)
            out_copy(2 * p).start()
            out_copy(2 * p + 1).start()

        return carry

    def rest_of_kernel():
        kern_loads[1].wait()

    lax.fori_loop(0, 6, forward, 0)
    to_z(0)
    to_z(1)
    to_plane(3)
    lax.fori_loop(0, steps, flip, 0)
    to_z(2)
    to_gather(0)
    to_gather(1)
    to_z(3)
    to_gather(2)
    to_twin(0)
    to_twin(1)
    to_gather(3)
    weights_in(0)
    weights_in(1)
    halos_sent(stage, halo_send)
    remote(pair_in, pair_in, pair_send, pair_send, twin).wait_send()
    remote(xin, xin, x_send, x_send, twin).wait_send()
    remote(zin, zin, z_send, z_send, twin).wait_send()
    lax.fori_loop(0, 6, back, 0)
    remote(xin, xin, g_send, g_send, twin).wait_send()
    remote(xsend, xsend, p_send, p_send, twin).wait_send()
    lax.fori_loop(0, steps, finish, 0)
    halos_sent(edge_out, edge_send)
    pltpu.make_async_copy(sk, out_hbm.at[:, 0], out_sem).wait()


def split(mesh):
    bands, tiles = mesh.shape["band"], mesh.shape["tile"]
    if tiles == 64:
        return (bands // 2, 2, 4, 8)
    return (bands // 2, 1, tiles // 2, 2)


def body(sizes, sketch, diag_coef, couple, kernel, noise_prec):
    steps, _, rows, cols, width = sketch.shape
    sensors = kernel.shape[1]
    points = rows * cols
    nyl, nyh, nx, nz = sizes
    plane = nyl * nyh * nx
    tiles = nyh * nx * nz
    half = sensors // 2
    piece = half // plane
    chunks = steps // 2
    by_row = jnp.transpose(kernel, (0, 2, 3, 1, 4))
    diag_rows = jnp.transpose(diag_coef, (1, 0, 2))
    couple_rows = jnp.transpose(couple, (1, 0, 2))
    anywhere = pl.BlockSpec(memory_space=pl.ANY)

    def far(x):
        return pltpu.with_memory_space_constraint(x, pltpu.HBM)

    dma = pltpu.SemaphoreType.DMA
    sweep_scratch = [
        pltpu.VMEM((rows + 4, cols + 2 * PAD, width), F32),
        pltpu.VMEM((rows + 2, cols + 2 * PAD, width), F32),
        pltpu.VMEM((rows + 2, cols, width), F32),
    ]
    edge_shape = (steps, 2, 2 * cols, width)
    return pl.pallas_call(
        functools.partial(main_kernel, sizes),
        out_shape=jax.ShapeDtypeStruct(sketch.shape, F32),
        in_specs=[pl.BlockSpec(memory_space=pltpu.HBM)] * 5,
        out_specs=anywhere,
        scratch_shapes=[
            pltpu.VMEM(diag_rows.shape, F32),
            pltpu.VMEM(couple_rows.shape, F32),
            pltpu.VMEM(noise_prec.shape, F32),
            pltpu.VMEM((steps, rows, sensors, cols), BF16),
            pltpu.VMEM((steps, points, sensors), BF16),
            pltpu.VMEM((steps, rows, cols, width), F32),
            pltpu.VMEM((steps, rows, cols, width), F32),
            pltpu.VMEM(edge_shape, BF16),
            pltpu.VMEM(edge_shape, BF16),
            pltpu.VMEM((2, 2, chunks + 1, points, width), BF16),
            pltpu.VMEM((chunks, sensors, 2 * width), F32),
            pltpu.VMEM((chunks, half, 2 * width), F32),
            pltpu.VMEM((chunks, half, 2 * width), BF16),
            pltpu.VMEM((chunks, (plane - 1) * piece, 2 * width), BF16),
            pltpu.VMEM((chunks, piece, 2 * width), BF16),
            pltpu.VMEM((chunks, nz - 1, piece, 2 * width), BF16),
            pltpu.VMEM((chunks, 2, piece, width), BF16),
            pltpu.VMEM((2, 2, chunks + 2, sensors, width), BF16),
            pltpu.VMEM((steps, points, width), F32),
            pltpu.VMEM(edge_shape, BF16),
            pltpu.VMEM(edge_shape, BF16),
            pltpu.VMEM((2, 2, rows, 1, cols), F32),
            pltpu.VMEM((rows + 4, cols, width), F32),
            pltpu.VMEM((rows + 2, cols, width), F32),
            *sweep_scratch,
            dma((chunks + 5,)),
            dma((2,)), dma((2,)),
            dma((2,)), dma((steps, 2)),
            dma(()), dma((chunks,)),
            dma(()), dma((chunks,)),
            dma(()), dma((chunks,)),
            dma(()), dma((chunks,)),
            dma(()), dma((chunks,)),
            dma((2,)), dma((steps, 2)),
            dma(()),
        ],
        compiler_params=pltpu.CompilerParams(
            collective_id=0, has_side_effects=True, vmem_limit_bytes=48 * 1024 * 1024
        ),
        name="sketch_main",
    )(sketch, far(diag_rows), far(couple_rows), by_row, far(noise_prec))


def solution(mesh):
    placed = (
        P(None, "band", "tile", None, None),
        P("band", "tile", None),
        P("band", "tile", None),
        P(None, None, "band", "tile", None),
        P(),
    )
    return jax.shard_map(
        functools.partial(body, split(mesh)),
        mesh=mesh,
        in_specs=placed,
        out_specs=P(None, "band", "tile", None, None),
        check_vma=False,
    )
```

```python
import functools

import jax
import jax.numpy as jnp
from jax import lax
from jax.experimental import pallas as pl
from jax.experimental.pallas import tpu as pltpu
from jax.sharding import PartitionSpec as P

F32 = jnp.float32
BF16 = jnp.bfloat16
MESH = pl.DeviceIdType.MESH
COLS = 128
PAD = 8


def beside(ref, row):
    return ref[row, pl.ds(PAD - 1, COLS), :] + ref[row, pl.ds(PAD + 1, COLS), :]


def clear_pads(ref, rows):
    zero = jnp.zeros((PAD, ref.shape[2]), F32)
    for row in range(rows):
        ref[row, 0:PAD, :] = zero
        ref[row, PAD + COLS : 2 * PAD + COLS, :] = zero


def two_sweeps(rows, value, cpl, dia, coupled, again, swept, put):
    body = pl.ds(PAD, COLS)
    for j in range(rows + 4):
        coupled[j, body, :] = cpl[j] * value(j)
    for j in range(1, rows + 3):
        near = coupled[j - 1, body, :] + coupled[j + 1, body, :] + beside(coupled, j)
        once = dia[j - 1] * value(j) - cpl[j] * near
        swept[j - 1] = once
        again[j - 1, body, :] = cpl[j] * once
    for r in range(rows):
        q = r + 1
        near = again[q - 1, body, :] + again[q + 1, body, :] + beside(again, q)
        put(r, dia[q] * swept[q] - cpl[q + 1] * near)


class Place:
    def __init__(self, sizes):
        self.nyl, self.nyh, self.nx, self.nz = sizes
        self.tiles = self.nyh * self.nx * self.nz
        self.band = lax.axis_index("band")
        self.tile = lax.axis_index("tile")
        self.core = lax.rem(self.band, 2)
        self.z = lax.rem(self.tile, self.nz)
        self.plane = self.nyl * self.nyh * self.nx
        self.g = self.band // 2 * (self.nyh * self.nx) + self.tile // self.nz

    def twin(self):
        return (self.band + 1 - 2 * self.core, self.tile)

    def in_plane(self, d):
        sizes = (self.nyl, self.nyh, self.nx)
        inner = self.nyh * self.nx
        steps = (d // inner, d % inner // self.nx, d % self.nx)
        own = (self.g // inner, lax.rem(self.g, inner) // self.nx, lax.rem(self.g, self.nx))
        yl, yh, x = (lax.rem(o + step, n) for o, step, n in zip(own, steps, sizes))
        return yl * inner + yh * self.nx + x, (yl * 2 + self.core, (yh * self.nx + x) * self.nz + self.z)

    def plane_offsets(self):
        def hops(d):
            x = d % self.nx
            yl, yh = d // (self.nyh * self.nx), d // self.nx % self.nyh
            return min(x, self.nx - x) + (1 if yl else 2 * yh)

        return sorted(range(1, self.plane), key=hops, reverse=True)

    def z_offsets(self):
        return sorted(range(1, self.nz), key=lambda d: min(d, self.nz - d), reverse=True)

    def along_z(self, d):
        z = lax.rem(self.z + d, self.nz)
        return (self.band, self.tile - self.z + z)

    def row_neighbour(self, step):
        return (self.band, lax.rem(self.tile + step + self.tiles, self.tiles))


def remote(src, dst, send, recv, where):
    return pltpu.make_async_remote_copy(
        src_ref=src, dst_ref=dst, send_sem=send, recv_sem=recv, device_id=where, device_id_type=MESH
    )


def main_kernel(
    sizes,
    sketch_hbm, diag_hbm, couple_hbm, kern_hbm, prec_hbm,
    out_ref,
    diag_ref, couple_ref, prec_ref,
    kv, kt, sk, field, stage, hin, smooth, total, pair_in, xsend, xin, zsend, zin, wsend, wgt, adj,
    edge_out, edge_in, coef_in, cpl, dia, coupled, again, swept,
    load_sem, coef_send, coef_recv, halo_send, halo_recv, pair_send, pair_recv, x_send, x_recv,
    z_send, z_recv, g_send, g_recv, p_send, p_recv, edge_send, edge_recv,
):
    here = Place(sizes)
    steps, rows, sensors, _ = kv.shape
    points = rows * COLS
    chunks = steps // 2
    pairs = steps // 2
    half = sensors // 2
    piece = half // here.plane
    others = here.plane - 1
    zothers = here.nz - 1
    up, down = here.row_neighbour(-1), here.row_neighbour(1)
    has_up, has_down = here.tile > 0, here.tile < here.tiles - 1
    twin = here.twin()

    sketch_loads = [
        pltpu.make_async_copy(sketch_hbm.at[2 * p : 2 * p + 2, 0], sk.at[2 * p : 2 * p + 2], load_sem.at[p])
        for p in range(pairs)
    ]
    kern_loads = [
        pltpu.make_async_copy(kern_hbm.at[lag : lag + 4, 0], kv.at[lag : lag + 4], load_sem.at[pairs + i])
        for i, lag in enumerate(range(0, steps, 4))
    ]
    small_loads = [
        pltpu.make_async_copy(src, dst, load_sem.at[pairs + 2 + i])
        for i, (src, dst) in enumerate(
            ((couple_hbm, couple_ref), (diag_hbm, diag_ref), (prec_hbm, prec_ref))
        )
    ]
    barrier = pltpu.get_barrier_semaphore()
    greeted = [up, down, twin]
    greeted += [here.in_plane(d)[1] for d in range(1, here.plane)]
    greeted += [here.along_z(d) for d in range(1, here.nz)]
    for load in sketch_loads:
        load.start()
    for where in greeted:
        pl.semaphore_signal(barrier, inc=1, device_id=where, device_id_type=MESH)
    for load in small_loads + kern_loads:
        load.start()

    low = lax.broadcasted_iota(jnp.int32, (COLS, COLS), 1) < COLS // 2

    def turn(x):
        return pltpu.roll(x, COLS // 2, 1)

    def coef_copies(side, where):
        return [
            remote(ref, coef_in.at[side, i], coef_send.at[side], coef_recv.at[side], where)
            for i, ref in enumerate((couple_hbm, diag_hbm))
        ]

    def coef_bulk(side, where):
        return remote(coef_in.at[side], coef_in.at[side], coef_send.at[side], coef_recv.at[side], where)

    def halo_copy(f, side, where):
        return remote(
            stage.at[f, 1 - side], hin.at[f, side], halo_send.at[side], halo_recv.at[f, side], where
        )

    def edge_copy(f, side, where):
        return remote(
            edge_out.at[f, 1 - side], edge_in.at[f, side], edge_send.at[side], edge_recv.at[f, side], where
        )

    def send_halos(f, copy):
        @pl.when(has_up)
        def _():
            copy(f, 1, up).start()

        @pl.when(has_down)
        def _():
            copy(f, 0, down).start()

    def wait_halos(f, copy):
        @pl.when(has_up)
        def _():
            copy(f, 0, up).wait_recv()

        @pl.when(has_down)
        def _():
            copy(f, 1, down).wait_recv()

    def halos_sent(source, send):
        def one_side(side):
            block = source.at[:, 1 - side]
            remote(block, block, send.at[side], send.at[side], twin).wait_send()

        @pl.when(has_up)
        def _():
            one_side(1)

        @pl.when(has_down)
        def _():
            one_side(0)

    for p in range(pairs):
        sketch_loads[p].wait()

        for r in range(rows):
            first, second = sk[2 * p, r], sk[2 * p + 1, r]
            crossed = turn(jnp.where(low, second, first))
            field[p, r] = jnp.where(low, first, crossed)
            field[pairs + p, r] = jnp.where(low, crossed, second)
        for f in (p, pairs + p):
            stage[f, 0] = field[f, 0:2].reshape(2 * COLS, COLS).astype(BF16)
            stage[f, 1] = field[f, rows - 2 : rows].reshape(2 * COLS, COLS).astype(BF16)
        if p == 0:
            pl.semaphore_wait(barrier, len(greeted))

            @pl.when(has_up)
            def _():
                for copy in coef_copies(1, up):
                    copy.start()

            @pl.when(has_down)
            def _():
                for copy in coef_copies(0, down):
                    copy.start()

        send_halos(p, halo_copy)
    for p in range(pairs):
        send_halos(pairs + p, halo_copy)

    clear_pads(coupled, rows + 4)
    clear_pads(again, rows + 2)
    total[...] = jnp.zeros(total.shape, F32)
    adj[...] = jnp.zeros(adj.shape, F32)
    for h in range(2):
        smooth[h, 0, 0] = jnp.zeros((points, COLS), BF16)
        smooth[h, 1, 0] = jnp.zeros((points, COLS), BF16)
        wgt[h, 0, pairs] = jnp.zeros((sensors, COLS), BF16)
        wgt[h, 1, pairs + 1] = jnp.zeros((sensors, COLS), BF16)

    @pl.when(jnp.logical_not(has_up))
    def _():
        hin[:, 0] = jnp.zeros((steps, 2 * COLS, COLS), BF16)
        edge_in[:, 0] = jnp.zeros((steps, 2 * COLS, COLS), BF16)

    @pl.when(jnp.logical_not(has_down))
    def _():
        hin[:, 1] = jnp.zeros((steps, 2 * COLS, COLS), BF16)
        edge_in[:, 1] = jnp.zeros((steps, 2 * COLS, COLS), BF16)

    for load in small_loads:
        load.wait()

    def over_lanes(row):
        return jnp.broadcast_to(row, (COLS, COLS)).T

    for r in range(rows):
        cpl[r + 2] = over_lanes(couple_ref[r])
        dia[r + 1] = over_lanes(diag_ref[r])

    blank = jnp.zeros((COLS, COLS), F32)

    @pl.when(jnp.logical_not(has_up))
    def _():
        cpl[0] = blank
        cpl[1] = blank
        dia[0] = blank

    @pl.when(jnp.logical_not(has_down))
    def _():
        cpl[rows + 2] = blank
        cpl[rows + 3] = blank
        dia[rows + 1] = blank

    def flip(lag, carry):
        for r in range(rows):
            kt[lag, r * COLS : (r + 1) * COLS, :] = kv[lag, r].T
        return carry

    kern_loads[0].wait()

    @pl.when(has_up)
    def _():
        coef_bulk(0, up).wait_recv()
        coef_bulk(1, up).wait_send()
        cpl[0] = over_lanes(coef_in[0, 0, rows - 2])
        cpl[1] = over_lanes(coef_in[0, 0, rows - 1])
        dia[0] = over_lanes(coef_in[0, 1, rows - 1])

    @pl.when(has_down)
    def _():
        coef_bulk(1, down).wait_recv()
        coef_bulk(0, down).wait_send()
        cpl[rows + 2] = over_lanes(coef_in[1, 0, 0])
        cpl[rows + 3] = over_lanes(coef_in[1, 0, 1])
        dia[rows + 1] = over_lanes(coef_in[1, 1, 0])

    my_half = pl.multiple_of(here.core * half, half)
    twin_half = pl.multiple_of(half - here.core * half, half)
    my_piece = pl.multiple_of(here.g * piece, piece)
    my_sensors = pl.multiple_of(here.core * half + here.g * piece, piece)

    def rows_of(own, edges, f):
        def value(j):
            if j < 2:
                return edges[f, 0, j * COLS : (j + 1) * COLS, :].astype(F32)
            if j < rows + 2:
                return own(j - 2)
            j = j - rows - 2
            return edges[f, 1, j * COLS : (j + 1) * COLS, :].astype(F32)

        return value

    def sweeps(value, put):
        two_sweeps(rows, value, cpl, dia, coupled, again, swept, put)

    def smooth_field(h, f):
        p = f - h * pairs
        wait_halos(f, halo_copy)

        def put(r, new):
            block = slice(r * COLS, (r + 1) * COLS)
            before = smooth[h, 0, p, block, :].astype(F32)
            smooth[h, 0, p + 1, block, :] = new.astype(BF16)
            smooth[h, 1, p + 1, block, :] = turn(jnp.where(low, new, before)).astype(BF16)

        sweeps(rows_of(lambda r: field[f, r], hin, f), put)

    def pair_copy(c):
        return remote(
            total.at[c, pl.ds(twin_half, half)], pair_in.at[c], pair_send, pair_recv.at[c], twin
        )

    def lags_dot(lags, lhs, rhs):
        left_side = jnp.concatenate([x for lag in lags for x in lhs(lag)], axis=1)
        right_side = jnp.concatenate([jnp.concatenate(rhs(lag), axis=1) for lag in lags], axis=0)
        return jnp.dot(left_side, right_side, preferred_element_type=F32)

    def at_step(step, wanted, *actions):
        @pl.when(step == wanted)
        def _():
            for action in actions:
                action()

    def forward(k, carry):
        h, i = k // 3, lax.rem(k, 3)
        q = (i + 1) // 2
        c = 2 * h + q
        fresh = i != 1
        start = jnp.where(fresh, 0, 4)

        at_step(k, 1, rest_of_kernel)
        at_step(k, 3, lambda: to_plane(0))

        @pl.when(fresh)
        def _():
            def per_field(f, inner):
                smooth_field(h, f)
                return inner

            lax.fori_loop(2 * c, 2 * c + 2, per_field, 0)

        at_step(k, 3, lambda: to_plane(1))
        at_step(k, 5, lambda: to_plane(2))
        first = 2 * q + 1 - start // 2

        def lhs(lag):
            return [kv[start + lag, r] for r in range(rows)]

        def rhs(lag):
            odd, at = lag % 2, first - lag // 2
            return [smooth[h, odd, at], smooth[h, odd, at + 1]]

        total[c] += lags_dot(range(4), lhs, rhs)

        @pl.when(fresh)
        def _():
            pair_copy(c).start()

        return carry

    def plane_copies(c):
        copies = []
        for d in here.plane_offsets():
            g, where = here.in_plane(d)
            copies.append(
                remote(
                    xsend.at[c, pl.ds(pl.multiple_of(g * piece, piece), piece)],
                    xin.at[c, pl.ds((d - 1) * piece, piece)],
                    x_send, x_recv.at[c], where,
                )
            )
        return copies

    def bulk(c, send, recv):
        block = xin.at[c]
        return remote(block, block, send, recv, twin)

    def to_plane(c):
        pair_copy(c).wait_recv()
        xsend[c] = (total[c, pl.ds(my_half, half)] + pair_in[c]).astype(BF16)
        for copy in plane_copies(c):
            copy.start()

    def z_copies(c):
        return [
            remote(zsend.at[c], zin.at[c, d - 1], z_send, z_recv.at[c], here.along_z(d))
            for d in here.z_offsets()
        ]

    def own_sum(c):
        rows_here = pl.ds(pl.multiple_of(my_half + my_piece, piece), piece)
        acc = total[c, rows_here] + pair_in[c, pl.ds(my_piece, piece)]
        for d in range(others):
            acc = acc + xin[c, d * piece : (d + 1) * piece].astype(F32)
        return acc

    def to_z(c):
        bulk(c, x_send, x_recv.at[c]).wait_recv()
        zsend[c] = own_sum(c).astype(BF16)
        for copy in z_copies(c):
            copy.start()

    def gather_copies(c):
        h, q = c // 2, c % 2
        return [
            remote(
                wsend.at[c],
                wgt.at[h, 0, pl.ds(2 * q, 2), pl.ds(my_sensors, piece)],
                g_send, g_recv.at[c], here.in_plane(d)[1],
            )
            for d in here.plane_offsets()
        ]

    spot = lax.broadcasted_iota(jnp.int32, (piece, sensors), 1)
    wanted = lax.broadcasted_iota(jnp.int32, (piece, sensors), 0) + my_sensors
    left = lax.broadcasted_iota(jnp.int32, (piece, COLS), 1) < COLS // 2

    def scale_of(t):
        return jnp.sum(jnp.where(spot == wanted, prec_ref[t : t + 1, :], 0.0), axis=1, keepdims=True)

    def to_gather(c):
        h, q = c // 2, c % 2
        remote(zin.at[c], zin.at[c], z_send, z_recv.at[c], twin).wait_recv()
        acc = own_sum(c)
        for d in range(zothers):
            acc = acc + zin[c, d].astype(F32)
        for i in range(2):
            t = 4 * q + 2 * i
            scale = jnp.where(left, scale_of(t), scale_of(t + 1))
            block = (acc[:, i * COLS : (i + 1) * COLS] * scale).astype(BF16)
            wsend[c, i] = block
            wgt[h, 0, 2 * q + i, pl.ds(my_sensors, piece), :] = block
        for copy in gather_copies(c):
            copy.start()

    def twin_copy(c):
        h, q = c // 2, c % 2
        block = wgt.at[h, 0, pl.ds(2 * q, 2), pl.ds(my_half, half)]
        return remote(block, block, p_send, p_recv.at[c], twin)

    def shift_blocks(c, base):
        h, q = c // 2, c % 2
        for p in (2, 3, 4) if q else (1,):
            for s in range(0, half, min(half, COLS)):
                block = pl.ds(pl.multiple_of(base + s, piece), min(half, COLS))
                mixed = jnp.where(
                    low[: min(half, COLS)],
                    wgt[h, 0, p, block, :].astype(F32),
                    wgt[h, 0, p - 1, block, :].astype(F32),
                )
                wgt[h, 1, p, block, :] = turn(mixed).astype(BF16)

    def to_twin(c):
        bulk(c, g_send, g_recv.at[c]).wait_recv()
        twin_copy(c).start()
        shift_blocks(c, my_half)

    def weights_in(c):
        twin_copy(c).wait_recv()
        shift_blocks(c, twin_half)

    def back(k, carry):
        h, i = k // 3, lax.rem(k, 3)
        q = jnp.where(i == 0, 1, 0)
        c = 2 * h + q
        start = jnp.where(i == 2, 4, 0)
        at_step(k, 2, lambda: to_twin(2))
        at_step(k, 3, lambda: to_twin(3), lambda: weights_in(2), lambda: weights_in(3))
        first = 2 * q + start // 2

        def lhs(lag):
            return [kt[start + lag]]

        def rhs(lag):
            odd, at = lag % 2, first + (lag + 1) // 2
            return [wgt[h, odd, at], wgt[h, odd, at + 1]]

        out = lags_dot(range(4), lhs, rhs)
        adj[2 * c] += out[:, :COLS]
        adj[2 * c + 1] += out[:, COLS:]

        @pl.when(i != 1)
        def _():
            for f in (2 * c, 2 * c + 1):
                edge_out[f, 0] = adj[f, 0 : 2 * COLS, :].astype(BF16)
                edge_out[f, 1] = adj[f, points - 2 * COLS : points, :].astype(BF16)
                send_halos(f, edge_copy)

        return carry

    def result(f):
        wait_halos(f, edge_copy)
        return rows_of(lambda r: adj[f, pl.ds(r * COLS, COLS), :], edge_in, f)

    def finish(k, carry):
        p = lax.rem(k + 2, pairs)
        f = k // pairs * pairs + p

        def put(r, new):
            field[f, r] = new

        sweeps(result(f), put)

        @pl.when(k >= pairs)
        def _():
            for r in range(rows):
                first, second = field[p, r], field[pairs + p, r]
                crossed = turn(jnp.where(low, second, first))
                out_ref[2 * p, 0, r] = jnp.where(low, first, crossed)
                out_ref[2 * p + 1, 0, r] = jnp.where(low, crossed, second)

        return carry

    def rest_of_kernel():
        kern_loads[1].wait()

    lax.fori_loop(0, 6, forward, 0)
    to_z(0)
    to_z(1)
    to_plane(3)
    lax.fori_loop(0, steps, flip, 0)
    to_z(2)
    to_gather(0)
    to_gather(1)
    to_z(3)
    to_gather(2)
    to_twin(0)
    to_twin(1)
    to_gather(3)
    weights_in(0)
    weights_in(1)
    halos_sent(stage, halo_send)
    remote(pair_in, pair_in, pair_send, pair_send, twin).wait_send()
    remote(xin, xin, x_send, x_send, twin).wait_send()
    remote(zin, zin, z_send, z_send, twin).wait_send()
    lax.fori_loop(0, 6, back, 0)
    remote(xin, xin, g_send, g_send, twin).wait_send()
    remote(xsend, xsend, p_send, p_send, twin).wait_send()
    lax.fori_loop(0, steps, finish, 0)
    halos_sent(edge_out, edge_send)


def split(mesh):
    bands, tiles = mesh.shape["band"], mesh.shape["tile"]
    if tiles == 64:
        return (bands // 2, 2, 4, 8)
    return (bands // 2, 1, tiles // 2, 2)


def body(sizes, sketch, diag_coef, couple, kernel, noise_prec):
    steps, _, rows, cols, width = sketch.shape
    sensors = kernel.shape[1]
    points = rows * cols
    nyl, nyh, nx, nz = sizes
    plane = nyl * nyh * nx
    tiles = nyh * nx * nz
    half = sensors // 2
    piece = half // plane
    chunks = steps // 2
    by_row = jnp.transpose(kernel, (0, 2, 3, 1, 4))
    diag_rows = jnp.transpose(diag_coef, (1, 0, 2))
    couple_rows = jnp.transpose(couple, (1, 0, 2))
    anywhere = pl.BlockSpec(memory_space=pl.ANY)

    def far(x):
        return pltpu.with_memory_space_constraint(x, pltpu.HBM)

    dma = pltpu.SemaphoreType.DMA
    sweep_scratch = [
        pltpu.VMEM((rows + 4, cols + 2 * PAD, width), F32),
        pltpu.VMEM((rows + 2, cols + 2 * PAD, width), F32),
        pltpu.VMEM((rows + 2, cols, width), F32),
    ]
    edge_shape = (steps, 2, 2 * cols, width)
    return pl.pallas_call(
        functools.partial(main_kernel, sizes),
        out_shape=jax.ShapeDtypeStruct(sketch.shape, F32),
        in_specs=[pl.BlockSpec(memory_space=pltpu.HBM)] * 5,
        out_specs=pl.BlockSpec(memory_space=pltpu.VMEM),
        scratch_shapes=[
            pltpu.VMEM(diag_rows.shape, F32),
            pltpu.VMEM(couple_rows.shape, F32),
            pltpu.VMEM(noise_prec.shape, F32),
            pltpu.VMEM((steps, rows, sensors, cols), BF16),
            pltpu.VMEM((steps, points, sensors), BF16),
            pltpu.VMEM((steps, rows, cols, width), F32),
            pltpu.VMEM((steps, rows, cols, width), F32),
            pltpu.VMEM(edge_shape, BF16),
            pltpu.VMEM(edge_shape, BF16),
            pltpu.VMEM((2, 2, chunks + 1, points, width), BF16),
            pltpu.VMEM((chunks, sensors, 2 * width), F32),
            pltpu.VMEM((chunks, half, 2 * width), F32),
            pltpu.VMEM((chunks, half, 2 * width), BF16),
            pltpu.VMEM((chunks, (plane - 1) * piece, 2 * width), BF16),
            pltpu.VMEM((chunks, piece, 2 * width), BF16),
            pltpu.VMEM((chunks, nz - 1, piece, 2 * width), BF16),
            pltpu.VMEM((chunks, 2, piece, width), BF16),
            pltpu.VMEM((2, 2, chunks + 2, sensors, width), BF16),
            pltpu.VMEM((steps, points, width), F32),
            pltpu.VMEM(edge_shape, BF16),
            pltpu.VMEM(edge_shape, BF16),
            pltpu.VMEM((2, 2, rows, 1, cols), F32),
            pltpu.VMEM((rows + 4, cols, width), F32),
            pltpu.VMEM((rows + 2, cols, width), F32),
            *sweep_scratch,
            dma((chunks + 5,)),
            dma((2,)), dma((2,)),
            dma((2,)), dma((steps, 2)),
            dma(()), dma((chunks,)),
            dma(()), dma((chunks,)),
            dma(()), dma((chunks,)),
            dma(()), dma((chunks,)),
            dma(()), dma((chunks,)),
            dma((2,)), dma((steps, 2)),
        ],
        compiler_params=pltpu.CompilerParams(
            collective_id=0, has_side_effects=True, vmem_limit_bytes=48 * 1024 * 1024
        ),
        name="sketch_main",
    )(sketch, far(diag_rows), far(couple_rows), by_row, far(noise_prec))


def solution(mesh):
    placed = (
        P(None, "band", "tile", None, None),
        P("band", "tile", None),
        P("band", "tile", None),
        P(None, None, "band", "tile", None),
        P(),
    )
    return jax.shard_map(
        functools.partial(body, split(mesh)),
        mesh=mesh,
        in_specs=placed,
        out_specs=P(None, "band", "tile", None, None),
        check_vma=False,
    )
```

```python
import functools

import jax
import jax.numpy as jnp
from jax import lax
from jax.experimental import pallas as pl
from jax.experimental.pallas import tpu as pltpu
from jax.sharding import PartitionSpec as P

F32 = jnp.float32
BF16 = jnp.bfloat16
MESH = pl.DeviceIdType.MESH
COLS = 128
PAD = 8


def beside(ref, row):
    return ref[row, pl.ds(PAD - 1, COLS), :] + ref[row, pl.ds(PAD + 1, COLS), :]


def clear_pads(ref, rows):
    zero = jnp.zeros((PAD, ref.shape[2]), F32)
    for row in range(rows):
        ref[row, 0:PAD, :] = zero
        ref[row, PAD + COLS : 2 * PAD + COLS, :] = zero


def two_sweeps(rows, value, cpl, dia, coupled, again, swept, put):
    body = pl.ds(PAD, COLS)
    for j in range(rows + 4):
        coupled[j, body, :] = cpl[j] * value(j)
    for j in range(1, rows + 3):
        near = coupled[j - 1, body, :] + coupled[j + 1, body, :] + beside(coupled, j)
        once = dia[j - 1] * value(j) - cpl[j] * near
        swept[j - 1] = once
        again[j - 1, body, :] = cpl[j] * once
    for r in range(rows):
        q = r + 1
        near = again[q - 1, body, :] + again[q + 1, body, :] + beside(again, q)
        put(r, dia[q] * swept[q] - cpl[q + 1] * near)


class Place:
    def __init__(self, sizes):
        self.nyl, self.nyh, self.nx, self.nz = sizes
        self.tiles = self.nyh * self.nx * self.nz
        self.band = lax.axis_index("band")
        self.tile = lax.axis_index("tile")
        self.core = lax.rem(self.band, 2)
        self.z = lax.rem(self.tile, self.nz)
        self.plane = self.nyl * self.nyh * self.nx
        self.g = self.band // 2 * (self.nyh * self.nx) + self.tile // self.nz

    def twin(self):
        return (self.band + 1 - 2 * self.core, self.tile)

    def in_plane(self, d):
        sizes = (self.nyl, self.nyh, self.nx)
        inner = self.nyh * self.nx
        steps = (d // inner, d % inner // self.nx, d % self.nx)
        own = (self.g // inner, lax.rem(self.g, inner) // self.nx, lax.rem(self.g, self.nx))
        yl, yh, x = (lax.rem(o + step, n) for o, step, n in zip(own, steps, sizes))
        return yl * inner + yh * self.nx + x, (yl * 2 + self.core, (yh * self.nx + x) * self.nz + self.z)

    def plane_offsets(self):
        def hops(d):
            x = d % self.nx
            yl, yh = d // (self.nyh * self.nx), d // self.nx % self.nyh
            return min(x, self.nx - x) + (1 if yl else 2 * yh)

        return sorted(range(1, self.plane), key=hops, reverse=True)

    def z_offsets(self):
        return sorted(range(1, self.nz), key=lambda d: min(d, self.nz - d), reverse=True)

    def along_z(self, d):
        z = lax.rem(self.z + d, self.nz)
        return (self.band, self.tile - self.z + z)

    def row_neighbour(self, step):
        return (self.band, lax.rem(self.tile + step + self.tiles, self.tiles))


def remote(src, dst, send, recv, where):
    return pltpu.make_async_remote_copy(
        src_ref=src, dst_ref=dst, send_sem=send, recv_sem=recv, device_id=where, device_id_type=MESH
    )


def main_kernel(
    sizes,
    sketch_hbm, diag_hbm, couple_hbm, kern_hbm, prec_hbm,
    out_ref,
    diag_ref, couple_ref, prec_ref,
    kv, kt, sk, field, stage, hin, smooth, total, pair_in, xsend, xin, zsend, zin, wsend, wgt, adj,
    edge_out, edge_in, coef_in, cpl, dia, coupled, again, swept,
    load_sem, coef_send, coef_recv, halo_send, halo_recv, pair_send, pair_recv, x_send, x_recv,
    z_send, z_recv, g_send, g_recv, p_send, p_recv, edge_send, edge_recv,
):
    here = Place(sizes)
    steps, rows, sensors, _ = kv.shape
    points = rows * COLS
    chunks = steps // 2
    pairs = steps // 2
    half = sensors // 2
    piece = half // here.plane
    others = here.plane - 1
    zothers = here.nz - 1
    up, down = here.row_neighbour(-1), here.row_neighbour(1)
    has_up, has_down = here.tile > 0, here.tile < here.tiles - 1
    twin = here.twin()

    sketch_loads = [
        pltpu.make_async_copy(sketch_hbm.at[2 * p : 2 * p + 2, 0], sk.at[2 * p : 2 * p + 2], load_sem.at[p])
        for p in range(pairs)
    ]
    kern_loads = [
        pltpu.make_async_copy(kern_hbm.at[lag : lag + 4, 0], kv.at[lag : lag + 4], load_sem.at[pairs + i])
        for i, lag in enumerate(range(0, steps, 4))
    ]
    small_loads = [
        pltpu.make_async_copy(src, dst, load_sem.at[pairs + 2 + i])
        for i, (src, dst) in enumerate(
            ((couple_hbm, couple_ref), (diag_hbm, diag_ref), (prec_hbm, prec_ref))
        )
    ]
    barrier = pltpu.get_barrier_semaphore()
    greeted = [up, down, twin]
    greeted += [here.in_plane(d)[1] for d in range(1, here.plane)]
    greeted += [here.along_z(d) for d in range(1, here.nz)]
    for load in sketch_loads:
        load.start()
    for where in greeted:
        pl.semaphore_signal(barrier, inc=1, device_id=where, device_id_type=MESH)
    for load in small_loads + kern_loads:
        load.start()

    low = lax.broadcasted_iota(jnp.int32, (COLS, COLS), 1) < COLS // 2

    def turn(x):
        return pltpu.roll(x, COLS // 2, 1)

    def coef_copies(side, where):
        return [
            remote(ref, coef_in.at[side, i], coef_send.at[side], coef_recv.at[side], where)
            for i, ref in enumerate((couple_hbm, diag_hbm))
        ]

    def coef_bulk(side, where):
        return remote(coef_in.at[side], coef_in.at[side], coef_send.at[side], coef_recv.at[side], where)

    def halo_copy(f, side, where):
        return remote(
            stage.at[f, 1 - side], hin.at[f, side], halo_send.at[side], halo_recv.at[f, side], where
        )

    def edge_copy(f, side, where):
        return remote(
            edge_out.at[f, 1 - side], edge_in.at[f, side], edge_send.at[side], edge_recv.at[f, side], where
        )

    def send_halos(f, copy):
        @pl.when(has_up)
        def _():
            copy(f, 1, up).start()

        @pl.when(has_down)
        def _():
            copy(f, 0, down).start()

    def wait_halos(f, copy):
        @pl.when(has_up)
        def _():
            copy(f, 0, up).wait_recv()

        @pl.when(has_down)
        def _():
            copy(f, 1, down).wait_recv()

    def halos_sent(source, send):
        def one_side(side):
            block = source.at[:, 1 - side]
            remote(block, block, send.at[side], send.at[side], twin).wait_send()

        @pl.when(has_up)
        def _():
            one_side(1)

        @pl.when(has_down)
        def _():
            one_side(0)

    for p in range(pairs):
        sketch_loads[p].wait()

        for r in range(rows):
            first, second = sk[2 * p, r], sk[2 * p + 1, r]
            crossed = turn(jnp.where(low, second, first))
            field[p, r] = jnp.where(low, first, crossed)
            field[pairs + p, r] = jnp.where(low, crossed, second)
        for f in (p, pairs + p):
            stage[f, 0] = field[f, 0:2].reshape(2 * COLS, COLS).astype(BF16)
            stage[f, 1] = field[f, rows - 2 : rows].reshape(2 * COLS, COLS).astype(BF16)
        if p == 0:
            pl.semaphore_wait(barrier, len(greeted))

            @pl.when(has_up)
            def _():
                for copy in coef_copies(1, up):
                    copy.start()

            @pl.when(has_down)
            def _():
                for copy in coef_copies(0, down):
                    copy.start()

        send_halos(p, halo_copy)
    for p in range(pairs):
        send_halos(pairs + p, halo_copy)

    clear_pads(coupled, rows + 4)
    clear_pads(again, rows + 2)
    total[...] = jnp.zeros(total.shape, F32)
    adj[...] = jnp.zeros(adj.shape, F32)
    for h in range(2):
        smooth[h, 0, 0] = jnp.zeros((points, COLS), BF16)
        smooth[h, 1, 0] = jnp.zeros((points, COLS), BF16)
        wgt[h, 0, pairs] = jnp.zeros((sensors, COLS), BF16)
        wgt[h, 1, pairs + 1] = jnp.zeros((sensors, COLS), BF16)

    @pl.when(jnp.logical_not(has_up))
    def _():
        hin[:, 0] = jnp.zeros((steps, 2 * COLS, COLS), BF16)
        edge_in[:, 0] = jnp.zeros((steps, 2 * COLS, COLS), BF16)

    @pl.when(jnp.logical_not(has_down))
    def _():
        hin[:, 1] = jnp.zeros((steps, 2 * COLS, COLS), BF16)
        edge_in[:, 1] = jnp.zeros((steps, 2 * COLS, COLS), BF16)

    for load in small_loads:
        load.wait()

    def over_lanes(row):
        return jnp.broadcast_to(row, (COLS, COLS)).T

    for r in range(rows):
        cpl[r + 2] = over_lanes(couple_ref[r])
        dia[r + 1] = over_lanes(diag_ref[r])

    blank = jnp.zeros((COLS, COLS), F32)

    @pl.when(jnp.logical_not(has_up))
    def _():
        cpl[0] = blank
        cpl[1] = blank
        dia[0] = blank

    @pl.when(jnp.logical_not(has_down))
    def _():
        cpl[rows + 2] = blank
        cpl[rows + 3] = blank
        dia[rows + 1] = blank

    def flip(lag, carry):
        for r in range(rows):
            kt[lag, r * COLS : (r + 1) * COLS, :] = kv[lag, r].T
        return carry

    kern_loads[0].wait()

    @pl.when(has_up)
    def _():
        coef_bulk(0, up).wait_recv()
        coef_bulk(1, up).wait_send()
        cpl[0] = over_lanes(coef_in[0, 0, rows - 2])
        cpl[1] = over_lanes(coef_in[0, 0, rows - 1])
        dia[0] = over_lanes(coef_in[0, 1, rows - 1])

    @pl.when(has_down)
    def _():
        coef_bulk(1, down).wait_recv()
        coef_bulk(0, down).wait_send()
        cpl[rows + 2] = over_lanes(coef_in[1, 0, 0])
        cpl[rows + 3] = over_lanes(coef_in[1, 0, 1])
        dia[rows + 1] = over_lanes(coef_in[1, 1, 0])

    my_half = pl.multiple_of(here.core * half, half)
    twin_half = pl.multiple_of(half - here.core * half, half)
    my_piece = pl.multiple_of(here.g * piece, piece)
    my_sensors = pl.multiple_of(here.core * half + here.g * piece, piece)

    def rows_of(own, edges, f):
        def value(j):
            if j < 2:
                return edges[f, 0, j * COLS : (j + 1) * COLS, :].astype(F32)
            if j < rows + 2:
                return own(j - 2)
            j = j - rows - 2
            return edges[f, 1, j * COLS : (j + 1) * COLS, :].astype(F32)

        return value

    def sweeps(value, put):
        two_sweeps(rows, value, cpl, dia, coupled, again, swept, put)

    def smooth_field(h, f):
        p = f - h * pairs
        wait_halos(f, halo_copy)

        def put(r, new):
            block = slice(r * COLS, (r + 1) * COLS)
            before = smooth[h, 0, p, block, :].astype(F32)
            smooth[h, 0, p + 1, block, :] = new.astype(BF16)
            smooth[h, 1, p + 1, block, :] = turn(jnp.where(low, new, before)).astype(BF16)

        sweeps(rows_of(lambda r: field[f, r], hin, f), put)

    def pair_copy(c):
        return remote(
            total.at[c, pl.ds(twin_half, half)], pair_in.at[c], pair_send, pair_recv.at[c], twin
        )

    def lags_dot(lags, lhs, rhs):
        left_side = jnp.concatenate([x for lag in lags for x in lhs(lag)], axis=1)
        right_side = jnp.concatenate([jnp.concatenate(rhs(lag), axis=1) for lag in lags], axis=0)
        return jnp.dot(left_side, right_side, preferred_element_type=F32)

    def at_step(step, wanted, *actions):
        @pl.when(step == wanted)
        def _():
            for action in actions:
                action()

    def forward(k, carry):
        h, i = k // 3, lax.rem(k, 3)
        q = (i + 1) // 2
        c = 2 * h + q
        fresh = i != 1
        start = jnp.where(fresh, 0, 4)

        at_step(k, 1, rest_of_kernel)
        at_step(k, 3, lambda: to_plane(0))

        @pl.when(fresh)
        def _():
            def per_field(f, inner):
                smooth_field(h, f)
                return inner

            lax.fori_loop(2 * c, 2 * c + 2, per_field, 0)

        at_step(k, 3, lambda: to_plane(1))
        at_step(k, 5, lambda: to_plane(2), lambda: to_z(0))
        first = 2 * q + 1 - start // 2

        def lhs(lag):
            return [kv[start + lag, r] for r in range(rows)]

        def rhs(lag):
            odd, at = lag % 2, first - lag // 2
            return [smooth[h, odd, at], smooth[h, odd, at + 1]]

        total[c] += lags_dot(range(4), lhs, rhs)

        @pl.when(fresh)
        def _():
            pair_copy(c).start()

        return carry

    def plane_copies(c):
        copies = []
        for d in here.plane_offsets():
            g, where = here.in_plane(d)
            copies.append(
                remote(
                    xsend.at[c, pl.ds(pl.multiple_of(g * piece, piece), piece)],
                    xin.at[c, pl.ds((d - 1) * piece, piece)],
                    x_send, x_recv.at[c], where,
                )
            )
        return copies

    def bulk(c, send, recv):
        block = xin.at[c]
        return remote(block, block, send, recv, twin)

    def to_plane(c):
        pair_copy(c).wait_recv()
        xsend[c] = (total[c, pl.ds(my_half, half)] + pair_in[c]).astype(BF16)
        for copy in plane_copies(c):
            copy.start()

    def z_copies(c):
        return [
            remote(zsend.at[c], zin.at[c, d - 1], z_send, z_recv.at[c], here.along_z(d))
            for d in here.z_offsets()
        ]

    def own_sum(c):
        rows_here = pl.ds(pl.multiple_of(my_half + my_piece, piece), piece)
        acc = total[c, rows_here] + pair_in[c, pl.ds(my_piece, piece)]
        for d in range(others):
            acc = acc + xin[c, d * piece : (d + 1) * piece].astype(F32)
        return acc

    def to_z(c):
        bulk(c, x_send, x_recv.at[c]).wait_recv()
        zsend[c] = own_sum(c).astype(BF16)
        for copy in z_copies(c):
            copy.start()

    def gather_copies(c):
        h, q = c // 2, c % 2
        return [
            remote(
                wsend.at[c],
                wgt.at[h, 0, pl.ds(2 * q, 2), pl.ds(my_sensors, piece)],
                g_send, g_recv.at[c], here.in_plane(d)[1],
            )
            for d in here.plane_offsets()
        ]

    spot = lax.broadcasted_iota(jnp.int32, (piece, sensors), 1)
    wanted = lax.broadcasted_iota(jnp.int32, (piece, sensors), 0) + my_sensors
    left = lax.broadcasted_iota(jnp.int32, (piece, COLS), 1) < COLS // 2

    def scale_of(t):
        return jnp.sum(jnp.where(spot == wanted, prec_ref[t : t + 1, :], 0.0), axis=1, keepdims=True)

    def to_gather(c):
        h, q = c // 2, c % 2
        remote(zin.at[c], zin.at[c], z_send, z_recv.at[c], twin).wait_recv()
        acc = own_sum(c)
        for d in range(zothers):
            acc = acc + zin[c, d].astype(F32)
        for i in range(2):
            t = 4 * q + 2 * i
            scale = jnp.where(left, scale_of(t), scale_of(t + 1))
            block = (acc[:, i * COLS : (i + 1) * COLS] * scale).astype(BF16)
            wsend[c, i] = block
            wgt[h, 0, 2 * q + i, pl.ds(my_sensors, piece), :] = block
        for copy in gather_copies(c):
            copy.start()

    def twin_copy(c):
        h, q = c // 2, c % 2
        block = wgt.at[h, 0, pl.ds(2 * q, 2), pl.ds(my_half, half)]
        return remote(block, block, p_send, p_recv.at[c], twin)

    def shift_blocks(c, base):
        h, q = c // 2, c % 2
        for p in (2, 3, 4) if q else (1,):
            for s in range(0, half, min(half, COLS)):
                block = pl.ds(pl.multiple_of(base + s, piece), min(half, COLS))
                mixed = jnp.where(
                    low[: min(half, COLS)],
                    wgt[h, 0, p, block, :].astype(F32),
                    wgt[h, 0, p - 1, block, :].astype(F32),
                )
                wgt[h, 1, p, block, :] = turn(mixed).astype(BF16)

    def to_twin(c):
        bulk(c, g_send, g_recv.at[c]).wait_recv()
        twin_copy(c).start()
        shift_blocks(c, my_half)

    def weights_in(c):
        twin_copy(c).wait_recv()
        shift_blocks(c, twin_half)

    def back(k, carry):
        h, i = k // 3, lax.rem(k, 3)
        q = jnp.where(i == 0, 1, 0)
        c = 2 * h + q
        start = jnp.where(i == 2, 4, 0)
        at_step(k, 2, lambda: to_twin(2))
        at_step(k, 3, lambda: to_twin(3), lambda: weights_in(2), lambda: weights_in(3))
        first = 2 * q + start // 2

        def lhs(lag):
            return [kt[start + lag]]

        def rhs(lag):
            odd, at = lag % 2, first + (lag + 1) // 2
            return [wgt[h, odd, at], wgt[h, odd, at + 1]]

        out = lags_dot(range(4), lhs, rhs)
        adj[2 * c] += out[:, :COLS]
        adj[2 * c + 1] += out[:, COLS:]

        @pl.when(i != 1)
        def _():
            for f in (2 * c, 2 * c + 1):
                edge_out[f, 0] = adj[f, 0 : 2 * COLS, :].astype(BF16)
                edge_out[f, 1] = adj[f, points - 2 * COLS : points, :].astype(BF16)
                send_halos(f, edge_copy)

        return carry

    def result(f):
        wait_halos(f, edge_copy)
        return rows_of(lambda r: adj[f, pl.ds(r * COLS, COLS), :], edge_in, f)

    def finish(k, carry):
        p = lax.rem(k + 2, pairs)
        f = k // pairs * pairs + p

        def put(r, new):
            field[f, r] = new

        sweeps(result(f), put)

        @pl.when(k >= pairs)
        def _():
            for r in range(rows):
                first, second = field[p, r], field[pairs + p, r]
                crossed = turn(jnp.where(low, second, first))
                out_ref[2 * p, 0, r] = jnp.where(low, first, crossed)
                out_ref[2 * p + 1, 0, r] = jnp.where(low, crossed, second)

        return carry

    def rest_of_kernel():
        kern_loads[1].wait()

    lax.fori_loop(0, 6, forward, 0)
    to_z(1)
    to_plane(3)
    lax.fori_loop(0, steps, flip, 0)
    to_z(2)
    to_gather(0)
    to_gather(1)
    to_z(3)
    to_gather(2)
    to_twin(0)
    to_twin(1)
    to_gather(3)
    weights_in(0)
    weights_in(1)
    halos_sent(stage, halo_send)
    remote(pair_in, pair_in, pair_send, pair_send, twin).wait_send()
    remote(xin, xin, x_send, x_send, twin).wait_send()
    remote(zin, zin, z_send, z_send, twin).wait_send()
    lax.fori_loop(0, 6, back, 0)
    remote(xin, xin, g_send, g_send, twin).wait_send()
    remote(xsend, xsend, p_send, p_send, twin).wait_send()
    lax.fori_loop(0, steps, finish, 0)
    halos_sent(edge_out, edge_send)


def split(mesh):
    bands, tiles = mesh.shape["band"], mesh.shape["tile"]
    if tiles == 64:
        return (bands // 2, 2, 4, 8)
    return (bands // 2, 1, tiles // 2, 2)


def body(sizes, sketch, diag_coef, couple, kernel, noise_prec):
    steps, _, rows, cols, width = sketch.shape
    sensors = kernel.shape[1]
    points = rows * cols
    nyl, nyh, nx, nz = sizes
    plane = nyl * nyh * nx
    tiles = nyh * nx * nz
    half = sensors // 2
    piece = half // plane
    chunks = steps // 2
    by_row = jnp.transpose(kernel, (0, 2, 3, 1, 4))
    diag_rows = jnp.transpose(diag_coef, (1, 0, 2))
    couple_rows = jnp.transpose(couple, (1, 0, 2))
    anywhere = pl.BlockSpec(memory_space=pl.ANY)

    def far(x):
        return pltpu.with_memory_space_constraint(x, pltpu.HBM)

    dma = pltpu.SemaphoreType.DMA
    sweep_scratch = [
        pltpu.VMEM((rows + 4, cols + 2 * PAD, width), F32),
        pltpu.VMEM((rows + 2, cols + 2 * PAD, width), F32),
        pltpu.VMEM((rows + 2, cols, width), F32),
    ]
    edge_shape = (steps, 2, 2 * cols, width)
    return pl.pallas_call(
        functools.partial(main_kernel, sizes),
        out_shape=jax.ShapeDtypeStruct(sketch.shape, F32),
        in_specs=[pl.BlockSpec(memory_space=pltpu.HBM)] * 5,
        out_specs=pl.BlockSpec(memory_space=pltpu.VMEM),
        scratch_shapes=[
            pltpu.VMEM(diag_rows.shape, F32),
            pltpu.VMEM(couple_rows.shape, F32),
            pltpu.VMEM(noise_prec.shape, F32),
            pltpu.VMEM((steps, rows, sensors, cols), BF16),
            pltpu.VMEM((steps, points, sensors), BF16),
            pltpu.VMEM((steps, rows, cols, width), F32),
            pltpu.VMEM((steps, rows, cols, width), F32),
            pltpu.VMEM(edge_shape, BF16),
            pltpu.VMEM(edge_shape, BF16),
            pltpu.VMEM((2, 2, chunks + 1, points, width), BF16),
            pltpu.VMEM((chunks, sensors, 2 * width), F32),
            pltpu.VMEM((chunks, half, 2 * width), F32),
            pltpu.VMEM((chunks, half, 2 * width), BF16),
            pltpu.VMEM((chunks, (plane - 1) * piece, 2 * width), BF16),
            pltpu.VMEM((chunks, piece, 2 * width), BF16),
            pltpu.VMEM((chunks, nz - 1, piece, 2 * width), BF16),
            pltpu.VMEM((chunks, 2, piece, width), BF16),
            pltpu.VMEM((2, 2, chunks + 2, sensors, width), BF16),
            pltpu.VMEM((steps, points, width), F32),
            pltpu.VMEM(edge_shape, BF16),
            pltpu.VMEM(edge_shape, BF16),
            pltpu.VMEM((2, 2, rows, 1, cols), F32),
            pltpu.VMEM((rows + 4, cols, width), F32),
            pltpu.VMEM((rows + 2, cols, width), F32),
            *sweep_scratch,
            dma((chunks + 5,)),
            dma((2,)), dma((2,)),
            dma((2,)), dma((steps, 2)),
            dma(()), dma((chunks,)),
            dma(()), dma((chunks,)),
            dma(()), dma((chunks,)),
            dma(()), dma((chunks,)),
            dma(()), dma((chunks,)),
            dma((2,)), dma((steps, 2)),
        ],
        compiler_params=pltpu.CompilerParams(
            collective_id=0, has_side_effects=True, vmem_limit_bytes=48 * 1024 * 1024
        ),
        name="sketch_main",
    )(sketch, far(diag_rows), far(couple_rows), by_row, far(noise_prec))


def solution(mesh):
    placed = (
        P(None, "band", "tile", None, None),
        P("band", "tile", None),
        P("band", "tile", None),
        P(None, None, "band", "tile", None),
        P(),
    )
    return jax.shard_map(
        functools.partial(body, split(mesh)),
        mesh=mesh,
        in_specs=placed,
        out_specs=P(None, "band", "tile", None, None),
        check_vma=False,
    )
```
